128 devices in a mesh: dp: 4 (over x), region: 32 (over y, z, core).
Axes of the slice: x: 4, y: 4, z: 4, core: 2. Of those that a mesh axis runs over, the one named last changes fastest.
Arguments:
- feats: bfloat16 [4, 32768, 256], P('dp', 'region'), may hold values from -6 to 6
- grad_out: bfloat16 [4, 32768, 256], P('dp', 'region'), may hold values from -6 to 6
- weight: bfloat16 [27, 256, 256], replicated, may hold values from -0.078125 to 0.078125
- loc_in: int32 [4, 32, 26, 256], P('dp', 'region'), may hold values from 0 to 1024, as said below
- loc_out: int32 [4, 32, 26, 256], P('dp', 'region'), may hold values from 0 to 1024, as said below
- bnd_out: int32 [4, 32, 2, 9, 128], P('dp', 'region'), may hold values from 0 to 1024, as said below
- bnd_in: int32 [4, 32, 2, 9, 128], P('dp', 'region'), may hold values from 0 to 1024, as said below
Outputs:
- grad_input: bfloat16 [4, 32768, 256], P('dp', 'region')
- grad_weight: float32 [27, 256, 256], replicated
The draws below stay inside these ranges and needn't reach their ends.
Inputs may be any that keep to these rules, and one draw needn't show every extreme that they name: `loc_in`: 1024 marks an empty slot; within one offset list of a block the live slots name distinct rows; a slot is empty in loc_in exactly where it is empty in loc_out. `loc_out`: 1024 marks an empty slot; within one offset list of a block the live slots name distinct rows. bnd_out[n, r, 1] is slot-aligned with bnd_in[n, r+1, 0], and bnd_out[n, r, 0] with bnd_in[n, r-1, 1] (n the scan, r the block): slot (f, b) of both names one pair, and it is empty (1024) in both together. Side 0 of the first block and side 1 of the last block are empty. Within one face list the live rows are distinct. `bnd_in`: aligned with bnd_out as stated there; within one face list the live rows are distinct.
All inputs are finite; a program needn't handle non-finite values.
Results may differ from the reference program's by a relative error of at most 0.0028.
Values may be sent and summed in bfloat16 or wider, within the bound.
A program may use at most 128 MiB of HBM per device.

```python
import math
import jax
import jax.numpy as jnp
from jax import lax

C = 256
VOX_DEV = 1024
PAIRS = 256
BPAIRS = 128
SCANS = 4
BLOCKS = 32
VOX = 32768


def first_rows(key_one, count):
    return jax.random.permutation(key_one, VOX_DEV)[:count].astype(jnp.int32)


def local_lists(key):
    base_key = jax.random.fold_in(key, 11)
    key_in, key_out, key_level, key_busy, key_trim = jax.random.split(base_key, 5)
    number = SCANS * BLOCKS * 26
    rows_in = jax.vmap(lambda kk: first_rows(kk, PAIRS))(jax.random.split(key_in, number)).reshape(SCANS, BLOCKS, 26, PAIRS)
    rows_out = jax.vmap(lambda kk: first_rows(kk, PAIRS))(jax.random.split(key_out, number)).reshape(SCANS, BLOCKS, 26, PAIRS)
    level = jax.random.randint(key_level, (SCANS, BLOCKS, 1), 1, 6)
    busiest = jax.random.randint(key_busy, (SCANS, 1, 1), 0, BLOCKS)
    level = jnp.where(jnp.arange(BLOCKS)[None, :, None] == busiest, 1, level)
    density = PAIRS // level
    density = jnp.broadcast_to(density, (SCANS, BLOCKS, 26))
    live = density - jax.random.randint(key_trim, (SCANS, BLOCKS, 26), 0, density // 4 + 1)
    used = jnp.arange(PAIRS)[None, None, None, :] < live[..., None]
    return (jnp.where(used, rows_in, VOX_DEV), jnp.where(used, rows_out, VOX_DEV))


def face_lists(key):
    base_key = jax.random.fold_in(key, 23)
    key_j, key_i, key_level, key_trim = jax.random.split(base_key, 4)
    links = BLOCKS - 1
    number = SCANS * links * 2 * 9
    rows_j = jax.vmap(lambda kk: first_rows(kk, BPAIRS))(jax.random.split(key_j, number)).reshape(SCANS, links, 2, 9, BPAIRS)
    rows_i = jax.vmap(lambda kk: first_rows(kk, BPAIRS))(jax.random.split(key_i, number)).reshape(SCANS, links, 2, 9, BPAIRS)
    level = jax.random.randint(key_level, (SCANS, links, 2, 1), 1, 6)
    density = jnp.broadcast_to(BPAIRS // level, (SCANS, links, 2, 9))
    live = density - jax.random.randint(key_trim, (SCANS, links, 2, 9), 0, density // 4 + 1)
    used = jnp.arange(BPAIRS)[None, None, None, None, :] < live[..., None]
    rows_j = jnp.where(used, rows_j, VOX_DEV)
    rows_i = jnp.where(used, rows_i, VOX_DEV)
    empty_list = jnp.full((SCANS, 1, 9, BPAIRS), VOX_DEV, jnp.int32)
    out_lower = jnp.concatenate([empty_list, rows_j[:, :, 1]], 1)
    out_upper = jnp.concatenate([rows_j[:, :, 0], empty_list], 1)
    in_lower = jnp.concatenate([empty_list, rows_i[:, :, 0]], 1)
    in_upper = jnp.concatenate([rows_i[:, :, 1], empty_list], 1)
    return (jnp.stack([out_lower, out_upper], 2), jnp.stack([in_lower, in_upper], 2))


def draw_loc_in(key, part):
    return local_lists(key)[0]


def draw_loc_out(key, part):
    return local_lists(key)[1]


def draw_bnd_out(key, part):
    return face_lists(key)[0]


def draw_bnd_in(key, part):
    return face_lists(key)[1]


def steps_of(rng, shape, pieces, smallest, largest):
    def one(dim, blocks):
        steps = jax.random.uniform(jax.random.fold_in(jax.random.fold_in(rng, 6), dim), (blocks,), jnp.float32, smallest / len(pieces), largest / len(pieces))
        return jnp.repeat(jnp.exp(steps), shape[dim] // blocks).reshape((-1,) + (1,) * (len(shape) - dim - 1))

    factor_of = one(*pieces[0])
    for cut in pieces[1:]:
        factor_of = factor_of * one(*cut)
    return factor_of


def bell_draw(own_key, dims, scale, limit, shards=(), held_as=jnp.bfloat16):
    factor_of = steps_of(own_key, dims, shards, -0.22, 0.18) if shards else 1.0
    values = jax.random.normal(own_key, dims, jnp.float32) * scale * factor_of
    return jnp.minimum(jnp.maximum(values, -limit), limit).astype(held_as)


def setup_inputs(seed: int = 0) -> dict:
    splits = jax.random.split(jax.random.key(seed), 8)
    feats = bell_draw(splits[0], (SCANS, VOX, C), 1.0, 6.0, ((0, 4), (1, 32)))
    grad_out = bell_draw(splits[1], (SCANS, VOX, C), 1.0, 6.0, ((0, 4), (1, 32)))
    weight = bell_draw(splits[2], (27, C, C), (27 * C) ** -0.5, 0.078125)
    loc_in = draw_loc_in(jax.random.fold_in(splits[7], 71), 0)
    loc_out = draw_loc_out(jax.random.fold_in(splits[7], 71), 0)
    bnd_out = draw_bnd_out(jax.random.fold_in(splits[7], 71), 0)
    bnd_in = draw_bnd_in(jax.random.fold_in(splits[7], 71), 0)
    return {"feats": feats, "grad_out": grad_out, "weight": weight, "loc_in": loc_in, "loc_out": loc_out, "bnd_out": bnd_out, "bnd_in": bnd_in}


def contract_rows(left, right):
    return lax.dot_general(left.astype(jnp.float32), right.astype(jnp.float32), (((0,), (0,)), ((), ())), precision=lax.Precision.HIGHEST)

def backward_rows(grads, kernel):
    return lax.dot_general(grads.astype(jnp.float32), kernel.astype(jnp.float32), (((1,), (1,)), ((), ())), precision=lax.Precision.HIGHEST)

def reference(feats, grad_out, weight, loc_in, loc_out, bnd_out, bnd_in):
    channels = feats.shape[2]
    blocks_all = SCANS * BLOCKS
    zero_rows = jnp.zeros((blocks_all, 1, channels), feats.dtype)
    feat_pad = jnp.concatenate([feats.reshape(blocks_all, VOX_DEV, channels), zero_rows], 1)
    grad_pad = jnp.concatenate([grad_out.reshape(blocks_all, VOX_DEV, channels), zero_rows], 1)
    local_in = loc_in.reshape(blocks_all, 26, PAIRS)
    local_out = loc_out.reshape(blocks_all, 26, PAIRS)
    face_out = bnd_out.reshape(blocks_all, 2, 9, BPAIRS)
    face_in = bnd_in.reshape(blocks_all, 2, 9, BPAIRS)

    def block_step(grad_total, block_index):
        position = block_index % BLOCKS
        lower_block = jnp.where(position > 0, block_index - 1, block_index)
        upper_block = jnp.where(position < BLOCKS - 1, block_index + 1, block_index)
        own_feat = feat_pad[block_index]
        own_grad = grad_pad[block_index]
        accumulated = backward_rows(own_grad, weight[13])
        grad_total = grad_total.at[13].add(contract_rows(own_feat, own_grad))

        def offset_step(carried, slot_index):
            acc_rows, totals = carried
            offset = slot_index + (slot_index >= 13).astype(jnp.int32)
            kernel = lax.dynamic_index_in_dim(weight, offset, 0, keepdims=False)
            rows_in = local_in[block_index, slot_index]
            rows_out = local_out[block_index, slot_index]
            gathered_x = own_feat[rows_in]
            gathered_g = own_grad[rows_out]
            acc_rows = acc_rows.at[rows_in].add(backward_rows(gathered_g, kernel))
            totals = totals.at[offset].add(contract_rows(gathered_x, gathered_g))
            return ((acc_rows, totals), None)
        (accumulated, grad_total), unused = lax.scan(offset_step, (accumulated, grad_total), jnp.arange(26).astype(jnp.int32))
        for face_side in range(2):
            source = lower_block if face_side == 0 else upper_block
            first_offset = 18 if face_side == 0 else 0
            rows_j = face_out[source, 1 - face_side]
            rows_i = face_in[block_index, face_side]
            grads_in = grad_pad[source][rows_j].astype(jnp.float32)
            feats_in = own_feat[rows_i].astype(jnp.float32)
            kernels = weight[first_offset:first_offset + 9].astype(jnp.float32)
            moved_rows = jnp.einsum('fbd,fcd->fbc', grads_in, kernels, precision=lax.Precision.HIGHEST).astype(jnp.bfloat16)
            moved_rows = lax.optimization_barrier(moved_rows).astype(jnp.float32)
            accumulated = accumulated.at[rows_i.reshape(-1)].add(moved_rows.reshape(-1, channels))
            grad_total = grad_total.at[first_offset:first_offset + 9].add(jnp.einsum('fbc,fbd->fcd', feats_in, grads_in, precision=lax.Precision.HIGHEST))
        return (grad_total, accumulated[:VOX_DEV].astype(jnp.bfloat16))
    initial = jnp.zeros((27, channels, channels), jnp.float32)
    grad_total, blocks_out = lax.scan(block_step, initial, jnp.arange(blocks_all).astype(jnp.int32))
    grad_input = blocks_out.reshape(SCANS, VOX_DEV * BLOCKS, channels)
    grad_weight = grad_total * (1.0 / math.sqrt(PAIRS * SCANS * BLOCKS))
    return (grad_input, grad_weight)
```

```python
import math

import jax
import jax.numpy as jnp
from jax import lax
from jax.sharding import PartitionSpec as P


GROUPS = {"core": ("region", 2), "z": ("region", 4), "y": ("region", 4), "x": ("dp", 4)}
COLOR_ORDERS = (("z", "y", "x"), ("y", "x", "z"), ("x", "z", "y"))


def rank_in(dim):
    if dim == "x":
        return lax.axis_index("dp")
    r = lax.axis_index("region")
    return {"y": r // 8, "z": (r // 2) % 4, "core": r % 2}[dim]


def shifted_pairs(dim, shift):
    if dim == "x":
        return [(i, (i + shift) % 4) for i in range(4)]
    pairs = []
    for r in range(32):
        y, z, c = r // 8, (r // 2) % 4, r % 2
        if dim == "y":
            y = (y + shift) % 4
        if dim == "z":
            z = (z + shift) % 4
        if dim == "core":
            c = (c + shift) % 2
        pairs.append((r, (y * 4 + z) * 2 + c))
    return pairs


def scatter_step(data, dim):
    axis, size = GROUPS[dim]
    me = rank_in(dim)
    data = data.reshape((size, data.shape[0] // size) + data.shape[1:])
    total = lax.dynamic_index_in_dim(data, me, 0, keepdims=False)
    for shift in range(1, size):
        send = lax.dynamic_index_in_dim(data, (me + shift) % size, 0, keepdims=False)
        total = total + lax.ppermute(send, axis, shifted_pairs(dim, shift))
    return total


def gather_step(piece, dim):
    axis, size = GROUPS[dim]
    me = rank_in(dim)
    parts = [piece] + [lax.ppermute(piece, axis, shifted_pairs(dim, s)) for s in range(1, size)]
    ordered = jnp.roll(jnp.stack(parts[::-1], 0), me + 1, axis=0)
    return ordered.reshape((size * piece.shape[0],) + piece.shape[1:])


def summed_everywhere(stacked):
    count = stacked.shape[0]
    colors = len(COLOR_ORDERS)
    rows = 40
    padded = colors * 128 * rows * 128
    flat = jnp.pad(stacked.reshape(-1), (0, padded - stacked.size))
    data = jnp.moveaxis(flat.reshape(colors, 128, rows, 128), 1, 0)
    data = scatter_step(data, "core")
    results = []
    for color, order in enumerate(COLOR_ORDERS):
        piece = data[:, color]
        for dim in order:
            piece = scatter_step(piece, dim)
        for dim in order[::-1]:
            piece = gather_step(piece, dim)
        results.append(piece)
    whole = gather_step(jnp.stack(results, 1), "core")
    whole = jnp.moveaxis(whole, 0, 1).reshape(-1)[: stacked.size]
    return whole.reshape(stacked.shape)


def passed_along(array, axis, by):
    peers = lax.axis_size(axis)
    pairs = [(i, i + by) for i in range(peers) if 0 <= i + by < peers]
    return lax.ppermute(array, axis, pairs)


def contract_rows(left, right):
    return lax.dot_general(
        left, right, (((0,), (0,)), ((), ())), preferred_element_type=jnp.float32
    )


def through_kernel(grads, kernel):
    return lax.dot_general(
        grads, kernel, (((1,), (1,)), ((), ())), preferred_element_type=jnp.float32
    )


def one_hot_rows(lists, rows_here):
    numbers = lax.broadcasted_iota(jnp.int32, lists.shape + (rows_here,), lists.ndim)
    return (lists[..., None] == numbers).astype(jnp.bfloat16)


def pick_rows(table, source):
    return jnp.einsum("...v,vc->...c", table, source, preferred_element_type=jnp.float32).astype(
        jnp.bfloat16
    )


def place_rows(table, rows):
    return jnp.einsum("fbv,fbc->vc", table, rows, preferred_element_type=jnp.float32)


def face_products(features, grads, kernels):
    weight_grad = jnp.einsum("fbc,fbd->fcd", features, grads, preferred_element_type=jnp.float32)
    out_rows = jnp.einsum(
        "fbd,fcd->fbc", grads, kernels, preferred_element_type=jnp.float32
    ).astype(jnp.bfloat16)
    return (weight_grad, out_rows)


def per_device(feats, grad_out, weight, loc_in, loc_out, bnd_out, bnd_in):
    rows_here = feats.shape[1]
    pairs = loc_in.shape[3]
    own_feat = feats[0]
    own_grad = grad_out[0]
    center = contract_rows(own_feat, own_grad)
    accumulated = through_kernel(own_grad, weight[13])
    table_in = one_hot_rows(loc_in[0, 0], rows_here)
    table_out = one_hot_rows(loc_out[0, 0], rows_here)
    gathered_x = pick_rows(table_in, own_feat)
    gathered_g = pick_rows(table_out, own_grad)
    placed = jnp.einsum(
        "kpv,kpc->vkc", table_in, gathered_g, preferred_element_type=jnp.float32
    ).astype(jnp.bfloat16)
    side_kernels = jnp.concatenate([weight[0:13], weight[14:27]], 0)
    accumulated = accumulated + jnp.einsum(
        "vkd,kcd->vc", placed, side_kernels, preferred_element_type=jnp.float32
    )
    offset_grads = jnp.einsum(
        "kpc,kpd->kcd", gathered_x, gathered_g, preferred_element_type=jnp.float32
    )
    low_kernels = weight[0:9]
    high_kernels = weight[18:27]
    face_out_table = one_hot_rows(bnd_out[0, 0], rows_here)
    face_in_table = one_hot_rows(bnd_in[0, 0], rows_here)
    own_grads = pick_rows(face_out_table, own_grad)
    asked = pick_rows(face_in_table, own_feat)
    fetched = [None, None]
    for face_side in range(2):
        fetched[1 - face_side] = passed_along(asked[face_side], "region", 2 * face_side - 1)
    low_grad, low_rows = face_products(fetched[0], own_grads[0], low_kernels)
    high_grad, high_rows = face_products(fetched[1], own_grads[1], high_kernels)
    outgoing = [low_rows, high_rows]
    for face_side in range(2):
        arrived = passed_along(outgoing[face_side], "region", 2 * face_side - 1)
        accumulated = accumulated + place_rows(face_in_table[1 - face_side], arrived)
    stacked = jnp.concatenate(
        [
            offset_grads[0:9] + low_grad,
            offset_grads[9:13],
            center[None],
            offset_grads[13:17],
            offset_grads[17:26] + high_grad,
        ],
        0,
    )
    loss_scale = 1.0 / math.sqrt(pairs * lax.axis_size("dp") * lax.axis_size("region"))
    summed = summed_everywhere(stacked)
    grad_weight = summed * loss_scale
    grad_input = accumulated.astype(jnp.bfloat16)[None]
    return (grad_input, grad_weight)


def solution(mesh):
    placed = (
        P("dp", "region", None),
        P("dp", "region", None),
        P(),
        P("dp", "region", None, None),
        P("dp", "region", None, None),
        P("dp", "region", None, None, None),
        P("dp", "region", None, None, None),
    )
    return jax.shard_map(
        per_device,
        mesh=mesh,
        in_specs=placed,
        out_specs=(P("dp", "region", None), P()),
        check_vma=False,
    )
```

```python
import functools
import math

import jax
import jax.numpy as jnp
from jax import lax
from jax.sharding import PartitionSpec as P

from jax.experimental import pallas as pl
from jax.experimental.pallas import tpu as pltpu

MESH_IDS = pl.DeviceIdType.MESH
COLOR_ORDERS = (("z", "y", "x"), ("y", "x", "z"), ("x", "z", "y"))
CHUNK_ROWS = 24
COLOR_ROWS = 128 * CHUNK_ROWS
PAD_OFFSETS = 36


def coords_here():
    r = lax.axis_index("region")
    return {"x": lax.axis_index("dp"), "y": r // 8, "z": (r // 2) % 4, "core": r % 2}


def peer_of(at, dim, shift):
    x, y, z, c = at["x"], at["y"], at["z"], at["core"]
    if dim == "x":
        x = (x + shift) % 4
    elif dim == "y":
        y = (y + shift) % 4
    elif dim == "z":
        z = (z + shift) % 4
    else:
        c = 1 - c
    return (x, (y * 4 + z) * 2 + c)


def add_rows(dst, first, others, rows, slab):
    def body(i, carry):
        at = pl.ds(pl.multiple_of(i * slab, slab), slab)
        total = first(at)
        for other in others:
            total = total + other(at)
        dst(at, total)
        return carry

    lax.fori_loop(0, rows // slab, body, 0)


def allreduce_kernel(scale, x_ref, out_ref, rcore, part, r1, p1, r2, p2, r3, red, gathered,
                     core_send, core_recv, rs_send, rs_recv, ag_send, ag_recv, agc_send, agc_recv, out_sem):
    at = coords_here()
    half = COLOR_ROWS // 2
    barrier = pltpu.get_barrier_semaphore()
    peers = [peer_of(at, "core", 1)] + [peer_of(at, d, s) for d in ("z", "y", "x") for s in (1, 2, 3)]
    for p in peers:
        pl.semaphore_signal(barrier, inc=1, device_id=p, device_id_type=MESH_IDS)
    pl.semaphore_wait(barrier, len(peers))

    c = at["core"]
    copies = []
    for k in range(3):
        cp = pltpu.make_async_remote_copy(
            src_ref=x_ref.at[pl.ds(pl.multiple_of(k * COLOR_ROWS + (1 - c) * half, 8), half)],
            dst_ref=rcore.at[k], send_sem=core_send.at[k], recv_sem=core_recv.at[k],
            device_id=peer_of(at, "core", 1), device_id_type=MESH_IDS)
        cp.start()
        copies.append(cp)
    for k in range(3):
        copies[k].wait()
        base = k * COLOR_ROWS + c * half
        add_rows(lambda a, v, k=k: part.__setitem__((k, a), v),
                 lambda a, base=base: x_ref[pl.ds(pl.multiple_of(base, 8) + a.start, a.size)],
                 [lambda a, k=k: rcore[k, a]], half, 128)

    sources = (part, p1, p2)
    recvs = (r1, r2, r3)
    blocks = (COLOR_ROWS // 8, COLOR_ROWS // 32, COLOR_ROWS // 128)
    ranks = [[at[d] for d in order] for order in COLOR_ORDERS]
    for stage in range(3):
        blk = blocks[stage]
        src, rbuf = sources[stage], recvs[stage]
        staged = []
        for k, order in enumerate(COLOR_ORDERS):
            dim = order[stage]
            me = ranks[k][stage]
            row = []
            for s in (1, 2, 3):
                cp = pltpu.make_async_remote_copy(
                    src_ref=src.at[k, pl.ds(pl.multiple_of(((me + s) % 4) * blk, 8), blk)],
                    dst_ref=rbuf.at[k, s - 1], send_sem=rs_send.at[stage, k, s - 1],
                    recv_sem=rs_recv.at[stage, k, s - 1],
                    device_id=peer_of(at, dim, s), device_id_type=MESH_IDS)
                cp.start()
                row.append(cp)
            staged.append(row)
        for k in range(3):
            for cp in staged[k]:
                cp.wait()
            me = ranks[k][stage]
            own = pl.multiple_of(me * blk, 8)
            others = [lambda a, k=k, j=j: rbuf[k, j, a] for j in range(3)]
            first = lambda a, k=k, own=own, src=src: src[k, pl.ds(own + a.start, a.size)]
            if stage == 0:
                add_rows(lambda a, v, k=k: p1.__setitem__((k, a), v), first, others, blk, 128)
            elif stage == 1:
                add_rows(lambda a, v, k=k: p2.__setitem__((k, a), v), first, others, blk, blk)
            else:
                total = first(pl.ds(0, blk)) + others[0](pl.ds(0, blk)) + others[1](pl.ds(0, blk)) + others[2](pl.ds(0, blk))
                a, b, e = ranks[k]
                pos = pl.multiple_of(k * COLOR_ROWS + (c * 64 + a * 16 + b * 4 + e) * CHUNK_ROWS, 8)
                gathered[pl.ds(pos, blk), :] = total * scale

    sizes = (COLOR_ROWS // 128, COLOR_ROWS // 32, COLOR_ROWS // 8)
    for step, stage in enumerate((2, 1, 0)):
        blk = sizes[step]
        staged = []
        for k, order in enumerate(COLOR_ORDERS):
            dim = order[stage]
            a, b, e = ranks[k]
            lead = (c * 64 + a * 16 + b * 4 + e, c * 64 + a * 16 + b * 4, c * 64 + a * 16)[step]
            pos = pl.multiple_of(k * COLOR_ROWS + lead * CHUNK_ROWS, 8)
            row = []
            for s in (1, 2, 3):
                cp = pltpu.make_async_remote_copy(
                    src_ref=gathered.at[pl.ds(pos, blk)], dst_ref=gathered.at[pl.ds(pos, blk)],
                    send_sem=ag_send.at[stage, k, s - 1], recv_sem=ag_recv.at[stage, k, s - 1],
                    device_id=peer_of(at, dim, s), device_id_type=MESH_IDS)
                cp.start()
                row.append(cp)
            staged.append(row)
        for row in staged:
            for cp in row:
                cp.wait()
    last = []
    for k in range(3):
        pos = pl.multiple_of(k * COLOR_ROWS + c * half, 8)
        cp = pltpu.make_async_remote_copy(
            src_ref=gathered.at[pl.ds(pos, half)], dst_ref=gathered.at[pl.ds(pos, half)],
            send_sem=agc_send.at[k], recv_sem=agc_recv.at[k],
            device_id=peer_of(at, "core", 1), device_id_type=MESH_IDS)
        cp.start()
        last.append(cp)
    for cp in last:
        cp.wait()
    done = pltpu.make_async_copy(gathered, out_ref, out_sem)
    done.start()
    done.wait()


def summed_everywhere(stacked, scale):
    rows = PAD_OFFSETS * 256
    width = stacked.shape[2]
    data = jnp.concatenate(
        [stacked, jnp.zeros((PAD_OFFSETS - stacked.shape[0],) + stacked.shape[1:], stacked.dtype)], 0
    ).reshape(rows, width)
    f32 = jnp.float32
    blocks = (COLOR_ROWS // 8, COLOR_ROWS // 32, COLOR_ROWS // 128)
    total = pl.pallas_call(
        functools.partial(allreduce_kernel, scale),
        out_shape=jax.ShapeDtypeStruct((rows, width), f32),
        in_specs=[pl.BlockSpec(memory_space=pltpu.VMEM)],
        out_specs=pl.BlockSpec(memory_space=pl.ANY),
        scratch_shapes=[
            pltpu.VMEM((3, COLOR_ROWS // 2, width), f32),
            pltpu.VMEM((3, COLOR_ROWS // 2, width), f32),
            pltpu.VMEM((3, 3, blocks[0], width), f32),
            pltpu.VMEM((3, blocks[0], width), f32),
            pltpu.VMEM((3, 3, blocks[1], width), f32),
            pltpu.VMEM((3, blocks[1], width), f32),
            pltpu.VMEM((3, 3, blocks[2], width), f32),
            pltpu.VMEM((3, blocks[2], width), f32),
            pltpu.VMEM((rows, width), f32),
            pltpu.SemaphoreType.DMA((3,)),
            pltpu.SemaphoreType.DMA((3,)),
            pltpu.SemaphoreType.DMA((3, 3, 3)),
            pltpu.SemaphoreType.DMA((3, 3, 3)),
            pltpu.SemaphoreType.DMA((3, 3, 3)),
            pltpu.SemaphoreType.DMA((3, 3, 3)),
            pltpu.SemaphoreType.DMA((3,)),
            pltpu.SemaphoreType.DMA((3,)),
            pltpu.SemaphoreType.DMA(()),
        ],
        compiler_params=pltpu.CompilerParams(
            collective_id=0, has_side_effects=True, vmem_limit_bytes=64 * 1024 * 1024
        ),
    )(data)
    return total[: stacked.shape[0] * stacked.shape[1]].reshape(stacked.shape)


def passed_along(array, axis, by):
    peers = lax.axis_size(axis)
    pairs = [(i, i + by) for i in range(peers) if 0 <= i + by < peers]
    return lax.ppermute(array, axis, pairs)


def contract_rows(left, right):
    return lax.dot_general(
        left, right, (((0,), (0,)), ((), ())), preferred_element_type=jnp.float32
    )


def through_kernel(grads, kernel):
    return lax.dot_general(
        grads, kernel, (((1,), (1,)), ((), ())), preferred_element_type=jnp.float32
    )


def one_hot_rows(lists, rows_here):
    numbers = lax.broadcasted_iota(jnp.int32, lists.shape + (rows_here,), lists.ndim)
    return (lists[..., None] == numbers).astype(jnp.bfloat16)


def pick_rows(table, source):
    return jnp.einsum("...v,vc->...c", table, source, preferred_element_type=jnp.float32).astype(
        jnp.bfloat16
    )


def place_rows(table, rows):
    return jnp.einsum("fbv,fbc->vc", table, rows, preferred_element_type=jnp.float32)


def face_products(features, grads, kernels):
    weight_grad = jnp.einsum("fbc,fbd->fcd", features, grads, preferred_element_type=jnp.float32)
    out_rows = jnp.einsum(
        "fbd,fcd->fbc", grads, kernels, preferred_element_type=jnp.float32
    ).astype(jnp.bfloat16)
    return (weight_grad, out_rows)


def per_device(feats, grad_out, weight, loc_in, loc_out, bnd_out, bnd_in):
    rows_here = feats.shape[1]
    pairs = loc_in.shape[3]
    own_feat = feats[0]
    own_grad = grad_out[0]
    center = contract_rows(own_feat, own_grad)
    accumulated = through_kernel(own_grad, weight[13])
    table_in = one_hot_rows(loc_in[0, 0], rows_here)
    table_out = one_hot_rows(loc_out[0, 0], rows_here)
    gathered_x = pick_rows(table_in, own_feat)
    gathered_g = pick_rows(table_out, own_grad)
    placed = jnp.einsum(
        "kpv,kpc->vkc", table_in, gathered_g, preferred_element_type=jnp.float32
    ).astype(jnp.bfloat16)
    side_kernels = jnp.concatenate([weight[0:13], weight[14:27]], 0)
    accumulated = accumulated + jnp.einsum(
        "vkd,kcd->vc", placed, side_kernels, preferred_element_type=jnp.float32
    )
    offset_grads = jnp.einsum(
        "kpc,kpd->kcd", gathered_x, gathered_g, preferred_element_type=jnp.float32
    )
    low_kernels = weight[0:9]
    high_kernels = weight[18:27]
    face_out_table = one_hot_rows(bnd_out[0, 0], rows_here)
    face_in_table = one_hot_rows(bnd_in[0, 0], rows_here)
    own_grads = pick_rows(face_out_table, own_grad)
    asked = pick_rows(face_in_table, own_feat)
    fetched = [None, None]
    for face_side in range(2):
        fetched[1 - face_side] = passed_along(asked[face_side], "region", 2 * face_side - 1)
    low_grad, low_rows = face_products(fetched[0], own_grads[0], low_kernels)
    high_grad, high_rows = face_products(fetched[1], own_grads[1], high_kernels)
    outgoing = [low_rows, high_rows]
    for face_side in range(2):
        arrived = passed_along(outgoing[face_side], "region", 2 * face_side - 1)
        accumulated = accumulated + place_rows(face_in_table[1 - face_side], arrived)
    stacked = jnp.concatenate(
        [
            offset_grads[0:9] + low_grad,
            offset_grads[9:13],
            center[None],
            offset_grads[13:17],
            offset_grads[17:26] + high_grad,
        ],
        0,
    )
    loss_scale = 1.0 / math.sqrt(pairs * lax.axis_size("dp") * lax.axis_size("region"))
    grad_weight = summed_everywhere(stacked, loss_scale)
    grad_input = accumulated.astype(jnp.bfloat16)[None]
    return (grad_input, grad_weight)


def solution(mesh):
    placed = (
        P("dp", "region", None),
        P("dp", "region", None),
        P(),
        P("dp", "region", None, None),
        P("dp", "region", None, None),
        P("dp", "region", None, None, None),
        P("dp", "region", None, None, None),
    )
    return jax.shard_map(
        per_device,
        mesh=mesh,
        in_specs=placed,
        out_specs=(P("dp", "region", None), P()),
        check_vma=False,
    )
```

```python
import functools
import math

import jax
import jax.numpy as jnp
from jax import lax
from jax.sharding import PartitionSpec as P

from jax.experimental import pallas as pl
from jax.experimental.pallas import tpu as pltpu

MESH_IDS = pl.DeviceIdType.MESH
COLOR_ORDERS = (("z", "y", "x"), ("y", "x", "z"), ("x", "z", "y"))
CHUNK_ROWS = 24
COLOR_ROWS = 128 * CHUNK_ROWS
PAD_OFFSETS = 36


def coords_here():
    r = lax.axis_index("region")
    return {"x": lax.axis_index("dp"), "y": r // 8, "z": (r // 2) % 4, "core": r % 2}


def peer_of(at, dim, shift):
    x, y, z, c = at["x"], at["y"], at["z"], at["core"]
    if dim == "x":
        x = (x + shift) % 4
    elif dim == "y":
        y = (y + shift) % 4
    elif dim == "z":
        z = (z + shift) % 4
    else:
        c = 1 - c
    return (x, (y * 4 + z) * 2 + c)


def add_rows(dst, first, others, rows, slab):
    def body(i, carry):
        at = pl.ds(pl.multiple_of(i * slab, slab), slab)
        total = first(at)
        for other in others:
            total = total + other(at)
        dst(at, total)
        return carry

    lax.fori_loop(0, rows // slab, body, 0)


def allreduce_kernel(scale, x_ref, out_ref, rcore, part, r1, p1, r2, p2, r3, red,
                     core_send, core_recv, rs_send, rs_recv, ag_send, ag_recv, agc_send, agc_recv, out_sem):
    at = coords_here()
    half = COLOR_ROWS // 2
    barrier = pltpu.get_barrier_semaphore()
    peers = [peer_of(at, "core", 1)] + [peer_of(at, d, s) for d in ("z", "y", "x") for s in (1, 2, 3)]
    for p in peers:
        pl.semaphore_signal(barrier, inc=1, device_id=p, device_id_type=MESH_IDS)
    pl.semaphore_wait(barrier, len(peers))

    c = at["core"]
    copies = []
    for k in range(3):
        cp = pltpu.make_async_remote_copy(
            src_ref=x_ref.at[pl.ds(pl.multiple_of(k * COLOR_ROWS + (1 - c) * half, 8), half)],
            dst_ref=rcore.at[k], send_sem=core_send.at[k], recv_sem=core_recv.at[k],
            device_id=peer_of(at, "core", 1), device_id_type=MESH_IDS)
        cp.start()
        copies.append(cp)
    for k in range(3):
        copies[k].wait()
        base = k * COLOR_ROWS + c * half
        add_rows(lambda a, v, k=k: part.__setitem__((k, a), v),
                 lambda a, base=base: x_ref[pl.ds(pl.multiple_of(base, 8) + a.start, a.size)],
                 [lambda a, k=k: rcore[k, a]], half, 128)

    sources = (part, p1, p2)
    recvs = (r1, r2, r3)
    blocks = (COLOR_ROWS // 8, COLOR_ROWS // 32, COLOR_ROWS // 128)
    ranks = [[at[d] for d in order] for order in COLOR_ORDERS]
    for stage in range(3):
        blk = blocks[stage]
        src, rbuf = sources[stage], recvs[stage]
        staged = []
        for k, order in enumerate(COLOR_ORDERS):
            dim = order[stage]
            me = ranks[k][stage]
            row = []
            for s in (1, 2, 3):
                cp = pltpu.make_async_remote_copy(
                    src_ref=src.at[k, pl.ds(pl.multiple_of(((me + s) % 4) * blk, 8), blk)],
                    dst_ref=rbuf.at[k, s - 1], send_sem=rs_send.at[stage, k, s - 1],
                    recv_sem=rs_recv.at[stage, k, s - 1],
                    device_id=peer_of(at, dim, s), device_id_type=MESH_IDS)
                cp.start()
                row.append(cp)
            staged.append(row)
        for k in range(3):
            for cp in staged[k]:
                cp.wait()
            me = ranks[k][stage]
            own = pl.multiple_of(me * blk, 8)
            others = [lambda a, k=k, j=j: rbuf[k, j, a] for j in range(3)]
            first = lambda a, k=k, own=own, src=src: src[k, pl.ds(own + a.start, a.size)]
            if stage == 0:
                add_rows(lambda a, v, k=k: p1.__setitem__((k, a), v), first, others, blk, 128)
            elif stage == 1:
                add_rows(lambda a, v, k=k: p2.__setitem__((k, a), v), first, others, blk, blk)
            else:
                total = first(pl.ds(0, blk)) + others[0](pl.ds(0, blk)) + others[1](pl.ds(0, blk)) + others[2](pl.ds(0, blk))
                a, b, e = ranks[k]
                pos = pl.multiple_of(k * COLOR_ROWS + (c * 64 + a * 16 + b * 4 + e) * CHUNK_ROWS, 8)
                red[k] = total * scale
                put = pltpu.make_async_copy(red.at[k], out_ref.at[pl.ds(pos, blk)], out_sem.at[k])
                put.start()
                put.wait()

    sizes = (COLOR_ROWS // 128, COLOR_ROWS // 32, COLOR_ROWS // 8)
    for step, stage in enumerate((2, 1, 0)):
        blk = sizes[step]
        staged = []
        for k, order in enumerate(COLOR_ORDERS):
            dim = order[stage]
            a, b, e = ranks[k]
            lead = (c * 64 + a * 16 + b * 4 + e, c * 64 + a * 16 + b * 4, c * 64 + a * 16)[step]
            pos = pl.multiple_of(k * COLOR_ROWS + lead * CHUNK_ROWS, 8)
            row = []
            for s in (1, 2, 3):
                cp = pltpu.make_async_remote_copy(
                    src_ref=out_ref.at[pl.ds(pos, blk)], dst_ref=out_ref.at[pl.ds(pos, blk)],
                    send_sem=ag_send.at[stage, k, s - 1], recv_sem=ag_recv.at[stage, k, s - 1],
                    device_id=peer_of(at, dim, s), device_id_type=MESH_IDS)
                cp.start()
                row.append(cp)
            staged.append(row)
        for row in staged:
            for cp in row:
                cp.wait()
    last = []
    for k in range(3):
        pos = pl.multiple_of(k * COLOR_ROWS + c * half, 8)
        cp = pltpu.make_async_remote_copy(
            src_ref=out_ref.at[pl.ds(pos, half)], dst_ref=out_ref.at[pl.ds(pos, half)],
            send_sem=agc_send.at[k], recv_sem=agc_recv.at[k],
            device_id=peer_of(at, "core", 1), device_id_type=MESH_IDS)
        cp.start()
        last.append(cp)
    for cp in last:
        cp.wait()


def summed_everywhere(stacked, scale):
    rows = PAD_OFFSETS * 256
    width = stacked.shape[2]
    data = jnp.concatenate(
        [stacked, jnp.zeros((PAD_OFFSETS - stacked.shape[0],) + stacked.shape[1:], stacked.dtype)], 0
    ).reshape(rows, width)
    f32 = jnp.float32
    blocks = (COLOR_ROWS // 8, COLOR_ROWS // 32, COLOR_ROWS // 128)
    total = pl.pallas_call(
        functools.partial(allreduce_kernel, scale),
        out_shape=jax.ShapeDtypeStruct((rows, width), f32),
        in_specs=[pl.BlockSpec(memory_space=pltpu.VMEM)],
        out_specs=pl.BlockSpec(memory_space=pl.ANY),
        scratch_shapes=[
            pltpu.VMEM((3, COLOR_ROWS // 2, width), f32),
            pltpu.VMEM((3, COLOR_ROWS // 2, width), f32),
            pltpu.VMEM((3, 3, blocks[0], width), f32),
            pltpu.VMEM((3, blocks[0], width), f32),
            pltpu.VMEM((3, 3, blocks[1], width), f32),
            pltpu.VMEM((3, blocks[1], width), f32),
            pltpu.VMEM((3, 3, blocks[2], width), f32),
            pltpu.VMEM((3, blocks[2], width), f32),
            pltpu.SemaphoreType.DMA((3,)),
            pltpu.SemaphoreType.DMA((3,)),
            pltpu.SemaphoreType.DMA((3, 3, 3)),
            pltpu.SemaphoreType.DMA((3, 3, 3)),
            pltpu.SemaphoreType.DMA((3, 3, 3)),
            pltpu.SemaphoreType.DMA((3, 3, 3)),
            pltpu.SemaphoreType.DMA((3,)),
            pltpu.SemaphoreType.DMA((3,)),
            pltpu.SemaphoreType.DMA((3,)),
        ],
        compiler_params=pltpu.CompilerParams(
            collective_id=0, has_side_effects=True, vmem_limit_bytes=64 * 1024 * 1024
        ),
    )(data)
    return total[: stacked.shape[0] * stacked.shape[1]].reshape(stacked.shape)


def passed_along(array, axis, by):
    peers = lax.axis_size(axis)
    pairs = [(i, i + by) for i in range(peers) if 0 <= i + by < peers]
    return lax.ppermute(array, axis, pairs)


def contract_rows(left, right):
    return lax.dot_general(
        left, right, (((0,), (0,)), ((), ())), preferred_element_type=jnp.float32
    )


def through_kernel(grads, kernel):
    return lax.dot_general(
        grads, kernel, (((1,), (1,)), ((), ())), preferred_element_type=jnp.float32
    )


def one_hot_rows(lists, rows_here):
    numbers = lax.broadcasted_iota(jnp.int32, lists.shape + (rows_here,), lists.ndim)
    return (lists[..., None] == numbers).astype(jnp.bfloat16)


def pick_rows(table, source):
    return jnp.einsum("...v,vc->...c", table, source, preferred_element_type=jnp.float32).astype(
        jnp.bfloat16
    )


def place_rows(table, rows):
    return jnp.einsum("fbv,fbc->vc", table, rows, preferred_element_type=jnp.float32)


def face_products(features, grads, kernels):
    weight_grad = jnp.einsum("fbc,fbd->fcd", features, grads, preferred_element_type=jnp.float32)
    out_rows = jnp.einsum(
        "fbd,fcd->fbc", grads, kernels, preferred_element_type=jnp.float32
    ).astype(jnp.bfloat16)
    return (weight_grad, out_rows)


def per_device(feats, grad_out, weight, loc_in, loc_out, bnd_out, bnd_in):
    rows_here = feats.shape[1]
    pairs = loc_in.shape[3]
    own_feat = feats[0]
    own_grad = grad_out[0]
    center = contract_rows(own_feat, own_grad)
    accumulated = through_kernel(own_grad, weight[13])
    table_in = one_hot_rows(loc_in[0, 0], rows_here)
    table_out = one_hot_rows(loc_out[0, 0], rows_here)
    gathered_x = pick_rows(table_in, own_feat)
    gathered_g = pick_rows(table_out, own_grad)
    placed = jnp.einsum(
        "kpv,kpc->vkc", table_in, gathered_g, preferred_element_type=jnp.float32
    ).astype(jnp.bfloat16)
    side_kernels = jnp.concatenate([weight[0:13], weight[14:27]], 0)
    accumulated = accumulated + jnp.einsum(
        "vkd,kcd->vc", placed, side_kernels, preferred_element_type=jnp.float32
    )
    offset_grads = jnp.einsum(
        "kpc,kpd->kcd", gathered_x, gathered_g, preferred_element_type=jnp.float32
    )
    low_kernels = weight[0:9]
    high_kernels = weight[18:27]
    face_out_table = one_hot_rows(bnd_out[0, 0], rows_here)
    face_in_table = one_hot_rows(bnd_in[0, 0], rows_here)
    own_grads = pick_rows(face_out_table, own_grad)
    asked = pick_rows(face_in_table, own_feat)
    fetched = [None, None]
    for face_side in range(2):
        fetched[1 - face_side] = passed_along(asked[face_side], "region", 2 * face_side - 1)
    low_grad, low_rows = face_products(fetched[0], own_grads[0], low_kernels)
    high_grad, high_rows = face_products(fetched[1], own_grads[1], high_kernels)
    outgoing = [low_rows, high_rows]
    for face_side in range(2):
        arrived = passed_along(outgoing[face_side], "region", 2 * face_side - 1)
        accumulated = accumulated + place_rows(face_in_table[1 - face_side], arrived)
    stacked = jnp.concatenate(
        [
            offset_grads[0:9] + low_grad,
            offset_grads[9:13],
            center[None],
            offset_grads[13:17],
            offset_grads[17:26] + high_grad,
        ],
        0,
    )
    loss_scale = 1.0 / math.sqrt(pairs * lax.axis_size("dp") * lax.axis_size("region"))
    grad_weight = summed_everywhere(stacked, loss_scale)
    grad_input = accumulated.astype(jnp.bfloat16)[None]
    return (grad_input, grad_weight)


def solution(mesh):
    placed = (
        P("dp", "region", None),
        P("dp", "region", None),
        P(),
        P("dp", "region", None, None),
        P("dp", "region", None, None),
        P("dp", "region", None, None, None),
        P("dp", "region", None, None, None),
    )
    return jax.shard_map(
        per_device,
        mesh=mesh,
        in_specs=placed,
        out_specs=(P("dp", "region", None), P()),
        check_vma=False,
    )
```

```python
import functools
import math

import jax
import jax.numpy as jnp
from jax import lax
from jax.sharding import PartitionSpec as P

from jax.experimental import pallas as pl
from jax.experimental.pallas import tpu as pltpu

MESH_IDS = pl.DeviceIdType.MESH
COLOR_ORDERS = (("z", "y", "x"), ("y", "x", "z"), ("x", "z", "y"))
CHUNK_ROWS = 24
COLOR_ROWS = 128 * CHUNK_ROWS
PAD_OFFSETS = 36


def coords_here():
    r = lax.axis_index("region")
    return {"x": lax.axis_index("dp"), "y": r // 8, "z": (r // 2) % 4, "core": r % 2}


def peer_of(at, dim, shift):
    x, y, z, c = at["x"], at["y"], at["z"], at["core"]
    if dim == "x":
        x = (x + shift) % 4
    elif dim == "y":
        y = (y + shift) % 4
    elif dim == "z":
        z = (z + shift) % 4
    else:
        c = 1 - c
    return (x, (y * 4 + z) * 2 + c)


def add_rows(dst, first, others, rows, slab):
    def body(i, carry):
        at = pl.ds(pl.multiple_of(i * slab, slab), slab)
        total = first(at)
        for other in others:
            total = total + other(at)
        dst(at, total)
        return carry

    lax.fori_loop(0, rows // slab, body, 0)


def allreduce_kernel(scale, x_ref, out_ref, rcore, part, r1, p1, r2, p2, r3, red,
                     core_send, core_recv, rs_send, rs_recv, ag_send, ag_recv, agc_send, agc_recv, out_sem):
    at = coords_here()
    half = COLOR_ROWS // 2
    barrier = pltpu.get_barrier_semaphore()
    peers = [peer_of(at, "core", 1)] + [peer_of(at, d, s) for d in ("z", "y", "x") for s in (1, 2, 3)]
    for p in peers:
        pl.semaphore_signal(barrier, inc=1, device_id=p, device_id_type=MESH_IDS)
    pl.semaphore_wait(barrier, len(peers))

    c = at["core"]
    copies = []
    for k in range(3):
        cp = pltpu.make_async_remote_copy(
            src_ref=x_ref.at[pl.ds(pl.multiple_of(k * COLOR_ROWS + (1 - c) * half, 8), half)],
            dst_ref=rcore.at[k], send_sem=core_send.at[k], recv_sem=core_recv.at[k],
            device_id=peer_of(at, "core", 1), device_id_type=MESH_IDS)
        cp.start()
        copies.append(cp)
    for k in range(3):
        copies[k].wait()
        base = k * COLOR_ROWS + c * half
        add_rows(lambda a, v, k=k: part.__setitem__((k, a), v),
                 lambda a, base=base: x_ref[pl.ds(pl.multiple_of(base, 8) + a.start, a.size)],
                 [lambda a, k=k: rcore[k, a]], half, 128)

    sources = (part, p1, p2)
    recvs = (r1, r2, r3)
    blocks = (COLOR_ROWS // 8, COLOR_ROWS // 32, COLOR_ROWS // 128)
    ranks = [[at[d] for d in order] for order in COLOR_ORDERS]
    for stage in range(3):
        blk = blocks[stage]
        src, rbuf = sources[stage], recvs[stage]
        staged = []
        for k, order in enumerate(COLOR_ORDERS):
            dim = order[stage]
            me = ranks[k][stage]
            row = []
            for s in (1, 2, 3):
                cp = pltpu.make_async_remote_copy(
                    src_ref=src.at[k, pl.ds(pl.multiple_of(((me + s) % 4) * blk, 8), blk)],
                    dst_ref=rbuf.at[k, s - 1], send_sem=rs_send.at[stage, k, s - 1],
                    recv_sem=rs_recv.at[stage, k, s - 1],
                    device_id=peer_of(at, dim, s), device_id_type=MESH_IDS)
                cp.start()
                row.append(cp)
            staged.append(row)
        for k in range(3):
            for cp in staged[k]:
                cp.wait()
            me = ranks[k][stage]
            own = pl.multiple_of(me * blk, 8)
            others = [lambda a, k=k, j=j: rbuf[k, j, a] for j in range(3)]
            first = lambda a, k=k, own=own, src=src: src[k, pl.ds(own + a.start, a.size)]
            if stage == 0:
                add_rows(lambda a, v, k=k: p1.__setitem__((k, a), v), first, others, blk, 128)
            elif stage == 1:
                add_rows(lambda a, v, k=k: p2.__setitem__((k, a), v), first, others, blk, blk)
            else:
                total = first(pl.ds(0, blk)) + others[0](pl.ds(0, blk)) + others[1](pl.ds(0, blk)) + others[2](pl.ds(0, blk))
                a, b, e = ranks[k]
                pos = pl.multiple_of(k * COLOR_ROWS + (c * 64 + a * 16 + b * 4 + e) * CHUNK_ROWS, 8)
                red[k] = total * scale
                put = pltpu.make_async_copy(red.at[k], out_ref.at[pl.ds(pos, blk)], out_sem.at[k])
                put.start()
                put.wait()

    sizes = (COLOR_ROWS // 128, COLOR_ROWS // 32, COLOR_ROWS // 8)
    for step, stage in enumerate((2, 1, 0)):
        blk = sizes[step]
        staged = []
        for k, order in enumerate(COLOR_ORDERS):
            dim = order[stage]
            a, b, e = ranks[k]
            lead = (c * 64 + a * 16 + b * 4 + e, c * 64 + a * 16 + b * 4, c * 64 + a * 16)[step]
            pos = pl.multiple_of(k * COLOR_ROWS + lead * CHUNK_ROWS, 8)
            row = []
            for s in (1, 2, 3):
                cp = pltpu.make_async_remote_copy(
                    src_ref=out_ref.at[pl.ds(pos, blk)], dst_ref=out_ref.at[pl.ds(pos, blk)],
                    send_sem=ag_send.at[stage, k, s - 1], recv_sem=ag_recv.at[stage, k, s - 1],
                    device_id=peer_of(at, dim, s), device_id_type=MESH_IDS)
                cp.start()
                row.append(cp)
            staged.append(row)
        for row in staged:
            for cp in row:
                cp.wait()
    last = []
    for k in range(3):
        pos = pl.multiple_of(k * COLOR_ROWS + c * half, 8)
        cp = pltpu.make_async_remote_copy(
            src_ref=out_ref.at[pl.ds(pos, half)], dst_ref=out_ref.at[pl.ds(pos, half)],
            send_sem=agc_send.at[k], recv_sem=agc_recv.at[k],
            device_id=peer_of(at, "core", 1), device_id_type=MESH_IDS)
        cp.start()
        last.append(cp)
    for cp in last:
        cp.wait()


def summed_everywhere(stacked, scale):
    rows = PAD_OFFSETS * 256
    width = stacked.shape[2]
    data = jnp.concatenate(
        [stacked, jnp.zeros((PAD_OFFSETS - stacked.shape[0],) + stacked.shape[1:], stacked.dtype)], 0
    ).reshape(rows, width)
    f32 = jnp.float32
    blocks = (COLOR_ROWS // 8, COLOR_ROWS // 32, COLOR_ROWS // 128)
    total = pl.pallas_call(
        functools.partial(allreduce_kernel, scale),
        out_shape=jax.ShapeDtypeStruct((rows, width), f32),
        in_specs=[pl.BlockSpec(memory_space=pltpu.VMEM)],
        out_specs=pl.BlockSpec(memory_space=pl.ANY),
        scratch_shapes=[
            pltpu.VMEM((3, COLOR_ROWS // 2, width), f32),
            pltpu.VMEM((3, COLOR_ROWS // 2, width), f32),
            pltpu.VMEM((3, 3, blocks[0], width), f32),
            pltpu.VMEM((3, blocks[0], width), f32),
            pltpu.VMEM((3, 3, blocks[1], width), f32),
            pltpu.VMEM((3, blocks[1], width), f32),
            pltpu.VMEM((3, 3, blocks[2], width), f32),
            pltpu.VMEM((3, blocks[2], width), f32),
            pltpu.SemaphoreType.DMA((3,)),
            pltpu.SemaphoreType.DMA((3,)),
            pltpu.SemaphoreType.DMA((3, 3, 3)),
            pltpu.SemaphoreType.DMA((3, 3, 3)),
            pltpu.SemaphoreType.DMA((3, 3, 3)),
            pltpu.SemaphoreType.DMA((3, 3, 3)),
            pltpu.SemaphoreType.DMA((3,)),
            pltpu.SemaphoreType.DMA((3,)),
            pltpu.SemaphoreType.DMA((3,)),
        ],
        compiler_params=pltpu.CompilerParams(
            collective_id=0, has_side_effects=True, vmem_limit_bytes=64 * 1024 * 1024
        ),
    )(data)
    return total[: stacked.shape[0] * stacked.shape[1]].reshape(stacked.shape)


def passed_along(array, axis, by):
    peers = lax.axis_size(axis)
    pairs = [(i, i + by) for i in range(peers) if 0 <= i + by < peers]
    return lax.ppermute(array, axis, pairs)


def contract_rows(left, right):
    return lax.dot_general(
        left, right, (((0,), (0,)), ((), ())), preferred_element_type=jnp.float32
    )


def through_kernel(grads, kernel):
    return lax.dot_general(
        grads, kernel, (((1,), (1,)), ((), ())), preferred_element_type=jnp.float32
    )


def one_hot_rows(lists, rows_here):
    numbers = lax.broadcasted_iota(jnp.int32, lists.shape + (rows_here,), lists.ndim)
    return (lists[..., None] == numbers).astype(jnp.bfloat16)


def pick_rows(table, source):
    return jnp.einsum("...v,vc->...c", table, source, preferred_element_type=jnp.float32).astype(
        jnp.bfloat16
    )


def place_rows(table, rows):
    return jnp.einsum("fbv,fbc->vc", table, rows, preferred_element_type=jnp.float32)


def face_products(features, grads, kernels):
    weight_grad = jnp.einsum("fbc,fbd->fcd", features, grads, preferred_element_type=jnp.float32)
    out_rows = jnp.einsum(
        "fbd,fcd->fbc", grads, kernels, preferred_element_type=jnp.float32
    ).astype(jnp.bfloat16)
    return (weight_grad, out_rows)


def per_device(feats, grad_out, weight, loc_in, loc_out, bnd_out, bnd_in):
    rows_here = feats.shape[1]
    pairs = loc_in.shape[3]
    own_feat = feats[0]
    own_grad = grad_out[0]
    center = contract_rows(own_feat, own_grad)
    accumulated = through_kernel(own_grad, weight[13])
    table_in = one_hot_rows(loc_in[0, 0], rows_here)
    table_out = one_hot_rows(loc_out[0, 0], rows_here)
    gathered_x = pick_rows(table_in, own_feat)
    gathered_g = pick_rows(table_out, own_grad)
    placed = jnp.einsum(
        "kpv,kpc->vkc", table_in, gathered_g, preferred_element_type=jnp.float32
    ).astype(jnp.bfloat16)
    side_kernels = jnp.concatenate([weight[0:13], weight[14:27]], 0)
    accumulated = accumulated + jnp.einsum(
        "vkd,kcd->vc", placed, side_kernels, preferred_element_type=jnp.float32
    )
    offset_grads = jnp.einsum(
        "kpc,kpd->kcd", gathered_x, gathered_g, preferred_element_type=jnp.float32
    )
    low_kernels = weight[0:9]
    high_kernels = weight[18:27]
    face_out_table = one_hot_rows(bnd_out[0, 0], rows_here)
    face_in_table = one_hot_rows(bnd_in[0, 0], rows_here)
    own_grads = pick_rows(face_out_table, own_grad)
    asked = pick_rows(face_in_table, own_feat)
    from_below = passed_along(own_grads[1], "region", 1)
    from_above = passed_along(own_grads[0], "region", -1)
    high_grad, below_rows = face_products(asked[0], from_below, high_kernels)
    low_grad, above_rows = face_products(asked[1], from_above, low_kernels)
    accumulated = accumulated + place_rows(face_in_table[0], below_rows)
    accumulated = accumulated + place_rows(face_in_table[1], above_rows)
    stacked = jnp.concatenate(
        [
            offset_grads[0:9] + low_grad,
            offset_grads[9:13],
            center[None],
            offset_grads[13:17],
            offset_grads[17:26] + high_grad,
        ],
        0,
    )
    loss_scale = 1.0 / math.sqrt(pairs * lax.axis_size("dp") * lax.axis_size("region"))
    grad_weight = summed_everywhere(stacked, loss_scale)
    grad_input = accumulated.astype(jnp.bfloat16)[None]
    return (grad_input, grad_weight)


def solution(mesh):
    placed = (
        P("dp", "region", None),
        P("dp", "region", None),
        P(),
        P("dp", "region", None, None),
        P("dp", "region", None, None),
        P("dp", "region", None, None, None),
        P("dp", "region", None, None, None),
    )
    return jax.shard_map(
        per_device,
        mesh=mesh,
        in_specs=placed,
        out_specs=(P("dp", "region", None), P()),
        check_vma=False,
    )
```

```python
import functools
import math

import jax
import jax.numpy as jnp
from jax import lax
from jax.sharding import PartitionSpec as P

from jax.experimental import pallas as pl
from jax.experimental.pallas import tpu as pltpu

MESH_IDS = pl.DeviceIdType.MESH
COLOR_ORDERS = (("z", "y", "x"), ("y", "x", "z"), ("x", "z", "y"))
CHUNK_ROWS = 24
COLOR_ROWS = 128 * CHUNK_ROWS
PAD_OFFSETS = 36


def coords_here():
    r = lax.axis_index("region")
    return {"x": lax.axis_index("dp"), "y": r // 8, "z": (r // 2) % 4, "core": r % 2}


def peer_of(at, dim, shift):
    x, y, z, c = at["x"], at["y"], at["z"], at["core"]
    if dim == "x":
        x = (x + shift) % 4
    elif dim == "y":
        y = (y + shift) % 4
    elif dim == "z":
        z = (z + shift) % 4
    else:
        c = 1 - c
    return (x, (y * 4 + z) * 2 + c)


def add_rows(dst, first, others, rows, slab):
    def body(i, carry):
        at = pl.ds(pl.multiple_of(i * slab, slab), slab)
        total = first(at)
        for other in others:
            total = total + other(at)
        dst(at, total)
        return carry

    lax.fori_loop(0, rows // slab, body, 0)


def allreduce_kernel(scale, x_ref, out_ref, rcore, part, r1, p1, r2, p2, r3, red,
                     core_send, core_recv, rs_send, rs_recv, ag_send, ag_recv, agc_send, agc_recv, out_sem):
    at = coords_here()
    half = COLOR_ROWS // 2
    barrier = pltpu.get_barrier_semaphore()
    peers = [peer_of(at, "core", 1)] + [peer_of(at, d, s) for d in ("z", "y", "x") for s in (1, 2, 3)]
    for p in peers:
        pl.semaphore_signal(barrier, inc=1, device_id=p, device_id_type=MESH_IDS)
    pl.semaphore_wait(barrier, len(peers))

    c = at["core"]
    copies = []
    for k in range(3):
        cp = pltpu.make_async_remote_copy(
            src_ref=x_ref.at[pl.ds(pl.multiple_of(k * COLOR_ROWS + (1 - c) * half, 8), half)],
            dst_ref=rcore.at[k], send_sem=core_send.at[k], recv_sem=core_recv.at[k],
            device_id=peer_of(at, "core", 1), device_id_type=MESH_IDS)
        cp.start()
        copies.append(cp)
    for k in range(3):
        copies[k].wait()
        base = k * COLOR_ROWS + c * half
        add_rows(lambda a, v, k=k: part.__setitem__((k, a), v),
                 lambda a, base=base: x_ref[pl.ds(pl.multiple_of(base, 8) + a.start, a.size)],
                 [lambda a, k=k: rcore[k, a]], half, 128)

    sources = (part, p1, p2)
    recvs = (r1, r2, r3)
    blocks = (COLOR_ROWS // 8, COLOR_ROWS // 32, COLOR_ROWS // 128)
    ranks = [[at[d] for d in order] for order in COLOR_ORDERS]
    for stage in range(3):
        blk = blocks[stage]
        src, rbuf = sources[stage], recvs[stage]
        staged = []
        for k, order in enumerate(COLOR_ORDERS):
            dim = order[stage]
            me = ranks[k][stage]
            row = []
            for s in (1, 2, 3):
                cp = pltpu.make_async_remote_copy(
                    src_ref=src.at[k, pl.ds(pl.multiple_of(((me + s) % 4) * blk, 8), blk)],
                    dst_ref=rbuf.at[k, s - 1], send_sem=rs_send.at[stage, k, s - 1],
                    recv_sem=rs_recv.at[stage, k, s - 1],
                    device_id=peer_of(at, dim, s), device_id_type=MESH_IDS)
                cp.start()
                row.append(cp)
            staged.append(row)
        for k in range(3):
            for cp in staged[k]:
                cp.wait()
            me = ranks[k][stage]
            own = pl.multiple_of(me * blk, 8)
            others = [lambda a, k=k, j=j: rbuf[k, j, a] for j in range(3)]
            first = lambda a, k=k, own=own, src=src: src[k, pl.ds(own + a.start, a.size)]
            if stage == 0:
                add_rows(lambda a, v, k=k: p1.__setitem__((k, a), v), first, others, blk, 128)
            elif stage == 1:
                add_rows(lambda a, v, k=k: p2.__setitem__((k, a), v), first, others, blk, blk)
            else:
                total = first(pl.ds(0, blk)) + others[0](pl.ds(0, blk)) + others[1](pl.ds(0, blk)) + others[2](pl.ds(0, blk))
                a, b, e = ranks[k]
                pos = pl.multiple_of(k * COLOR_ROWS + (c * 64 + a * 16 + b * 4 + e) * CHUNK_ROWS, 8)
                red[k] = total * scale
                put = pltpu.make_async_copy(red.at[k], out_ref.at[pl.ds(pos, blk)], out_sem.at[k])
                put.start()
                put.wait()

    sizes = (COLOR_ROWS // 128, COLOR_ROWS // 32, COLOR_ROWS // 8)
    for step, stage in enumerate((2, 1, 0)):
        blk = sizes[step]
        staged = []
        for k, order in enumerate(COLOR_ORDERS):
            dim = order[stage]
            a, b, e = ranks[k]
            lead = (c * 64 + a * 16 + b * 4 + e, c * 64 + a * 16 + b * 4, c * 64 + a * 16)[step]
            pos = pl.multiple_of(k * COLOR_ROWS + lead * CHUNK_ROWS, 8)
            row = []
            for s in (1, 2, 3):
                cp = pltpu.make_async_remote_copy(
                    src_ref=out_ref.at[pl.ds(pos, blk)], dst_ref=out_ref.at[pl.ds(pos, blk)],
                    send_sem=ag_send.at[stage, k, s - 1], recv_sem=ag_recv.at[stage, k, s - 1],
                    device_id=peer_of(at, dim, s), device_id_type=MESH_IDS)
                cp.start()
                row.append(cp)
            staged.append(row)
        for row in staged:
            for cp in row:
                cp.wait()
    last = []
    for k in range(3):
        pos = pl.multiple_of(k * COLOR_ROWS + c * half, 8)
        cp = pltpu.make_async_remote_copy(
            src_ref=out_ref.at[pl.ds(pos, half)], dst_ref=out_ref.at[pl.ds(pos, half)],
            send_sem=agc_send.at[k], recv_sem=agc_recv.at[k],
            device_id=peer_of(at, "core", 1), device_id_type=MESH_IDS)
        cp.start()
        last.append(cp)
    for cp in last:
        cp.wait()


def summed_everywhere(stacked, scale):
    rows = PAD_OFFSETS * 256
    width = stacked.shape[2]
    data = jnp.concatenate(
        [stacked, jnp.zeros((PAD_OFFSETS - stacked.shape[0],) + stacked.shape[1:], stacked.dtype)], 0
    ).reshape(rows, width)
    f32 = jnp.float32
    blocks = (COLOR_ROWS // 8, COLOR_ROWS // 32, COLOR_ROWS // 128)
    total = pl.pallas_call(
        functools.partial(allreduce_kernel, scale),
        out_shape=jax.ShapeDtypeStruct((rows, width), f32),
        in_specs=[pl.BlockSpec(memory_space=pltpu.VMEM)],
        out_specs=pl.BlockSpec(memory_space=pl.ANY),
        scratch_shapes=[
            pltpu.VMEM((3, COLOR_ROWS // 2, width), f32),
            pltpu.VMEM((3, COLOR_ROWS // 2, width), f32),
            pltpu.VMEM((3, 3, blocks[0], width), f32),
            pltpu.VMEM((3, blocks[0], width), f32),
            pltpu.VMEM((3, 3, blocks[1], width), f32),
            pltpu.VMEM((3, blocks[1], width), f32),
            pltpu.VMEM((3, 3, blocks[2], width), f32),
            pltpu.VMEM((3, blocks[2], width), f32),
            pltpu.SemaphoreType.DMA((3,)),
            pltpu.SemaphoreType.DMA((3,)),
            pltpu.SemaphoreType.DMA((3, 3, 3)),
            pltpu.SemaphoreType.DMA((3, 3, 3)),
            pltpu.SemaphoreType.DMA((3, 3, 3)),
            pltpu.SemaphoreType.DMA((3, 3, 3)),
            pltpu.SemaphoreType.DMA((3,)),
            pltpu.SemaphoreType.DMA((3,)),
            pltpu.SemaphoreType.DMA((3,)),
        ],
        compiler_params=pltpu.CompilerParams(
            collective_id=0, has_side_effects=True, vmem_limit_bytes=64 * 1024 * 1024
        ),
    )(data)
    return total[: stacked.shape[0] * stacked.shape[1]].reshape(stacked.shape)


def passed_along(array, axis, by):
    peers = lax.axis_size(axis)
    pairs = [(i, i + by) for i in range(peers) if 0 <= i + by < peers]
    return lax.ppermute(array, axis, pairs)


def contract_rows(left, right):
    return lax.dot_general(
        left, right, (((0,), (0,)), ((), ())), preferred_element_type=jnp.float32
    )


def through_kernel(grads, kernel):
    return lax.dot_general(
        grads, kernel, (((1,), (1,)), ((), ())), preferred_element_type=jnp.float32
    )


def one_hot_rows(lists, rows_here):
    numbers = lax.broadcasted_iota(jnp.int32, lists.shape + (rows_here,), lists.ndim)
    return (lists[..., None] == numbers).astype(jnp.bfloat16)


def take_rows(source, lists):
    padded = jnp.concatenate([source, jnp.zeros((1,) + source.shape[1:], source.dtype)], 0)
    picked = jnp.take(padded, lists.reshape(-1), axis=0, mode="clip")
    return picked.reshape(lists.shape + source.shape[1:])


def place_rows(table, rows):
    return jnp.einsum("fbv,fbc->vc", table, rows, preferred_element_type=jnp.float32)


def face_products(features, grads, kernels):
    weight_grad = jnp.einsum("fbc,fbd->fcd", features, grads, preferred_element_type=jnp.float32)
    out_rows = jnp.einsum(
        "fbd,fcd->fbc", grads, kernels, preferred_element_type=jnp.float32
    ).astype(jnp.bfloat16)
    return (weight_grad, out_rows)


def per_device(feats, grad_out, weight, loc_in, loc_out, bnd_out, bnd_in):
    rows_here = feats.shape[1]
    pairs = loc_in.shape[3]
    own_feat = feats[0]
    own_grad = grad_out[0]
    center = contract_rows(own_feat, own_grad)
    accumulated = through_kernel(own_grad, weight[13])
    table_in = one_hot_rows(loc_in[0, 0], rows_here)
    gathered_x = take_rows(own_feat, loc_in[0, 0])
    gathered_g = take_rows(own_grad, loc_out[0, 0])
    placed = jnp.einsum(
        "kpv,kpc->vkc", table_in, gathered_g, preferred_element_type=jnp.float32
    ).astype(jnp.bfloat16)
    side_kernels = jnp.concatenate([weight[0:13], weight[14:27]], 0)
    accumulated = accumulated + jnp.einsum(
        "vkd,kcd->vc", placed, side_kernels, preferred_element_type=jnp.float32
    )
    offset_grads = jnp.einsum(
        "kpc,kpd->kcd", gathered_x, gathered_g, preferred_element_type=jnp.float32
    )
    low_kernels = weight[0:9]
    high_kernels = weight[18:27]
    face_in_table = one_hot_rows(bnd_in[0, 0], rows_here)
    own_grads = take_rows(own_grad, bnd_out[0, 0])
    asked = take_rows(own_feat, bnd_in[0, 0])
    from_below = passed_along(own_grads[1], "region", 1)
    from_above = passed_along(own_grads[0], "region", -1)
    high_grad, below_rows = face_products(asked[0], from_below, high_kernels)
    low_grad, above_rows = face_products(asked[1], from_above, low_kernels)
    accumulated = accumulated + place_rows(face_in_table[0], below_rows)
    accumulated = accumulated + place_rows(face_in_table[1], above_rows)
    stacked = jnp.concatenate(
        [
            offset_grads[0:9] + low_grad,
            offset_grads[9:13],
            center[None],
            offset_grads[13:17],
            offset_grads[17:26] + high_grad,
        ],
        0,
    )
    loss_scale = 1.0 / math.sqrt(pairs * lax.axis_size("dp") * lax.axis_size("region"))
    grad_weight = summed_everywhere(stacked, loss_scale)
    grad_input = accumulated.astype(jnp.bfloat16)[None]
    return (grad_input, grad_weight)


def solution(mesh):
    placed = (
        P("dp", "region", None),
        P("dp", "region", None),
        P(),
        P("dp", "region", None, None),
        P("dp", "region", None, None),
        P("dp", "region", None, None, None),
        P("dp", "region", None, None, None),
    )
    return jax.shard_map(
        per_device,
        mesh=mesh,
        in_specs=placed,
        out_specs=(P("dp", "region", None), P()),
        check_vma=False,
    )
```

```python
import functools
import math

import jax
import jax.numpy as jnp
from jax import lax
from jax.sharding import PartitionSpec as P

from jax.experimental import pallas as pl
from jax.experimental.pallas import tpu as pltpu

MESH_IDS = pl.DeviceIdType.MESH
COLOR_ORDERS = (("z", "y", "x"), ("y", "x", "z"), ("x", "z", "y"))
CHUNK_ROWS = 24
COLOR_ROWS = 128 * CHUNK_ROWS
PAD_OFFSETS = 36


REAL_ROWS = 27 * 256


def real_chunk(color, lead):
    return color * COLOR_ROWS + lead * CHUNK_ROWS < REAL_ROWS


def coords_here():
    r = lax.axis_index("region")
    return {"x": lax.axis_index("dp"), "y": r // 8, "z": (r // 2) % 4, "core": r % 2}


def peer_of(at, dim, shift):
    x, y, z, c = at["x"], at["y"], at["z"], at["core"]
    if dim == "x":
        x = (x + shift) % 4
    elif dim == "y":
        y = (y + shift) % 4
    elif dim == "z":
        z = (z + shift) % 4
    else:
        c = 1 - c
    return (x, (y * 4 + z) * 2 + c)


def add_rows(dst, first, others, rows, slab):
    def body(i, carry):
        at = pl.ds(pl.multiple_of(i * slab, slab), slab)
        total = first(at)
        for other in others:
            total = total + other(at)
        dst(at, total)
        return carry

    lax.fori_loop(0, rows // slab, body, 0)


def allreduce_kernel(scale, x_ref, out_ref, rcore, part, r1, p1, r2, p2, r3, red,
                     core_send, core_recv, rs_send, rs_recv, ag_send, ag_recv, agc_send, agc_recv, out_sem):
    at = coords_here()
    half = COLOR_ROWS // 2
    barrier = pltpu.get_barrier_semaphore()
    peers = [peer_of(at, "core", 1)] + [peer_of(at, d, s) for d in ("z", "y", "x") for s in (1, 2, 3)]
    for p in peers:
        pl.semaphore_signal(barrier, inc=1, device_id=p, device_id_type=MESH_IDS)
    pl.semaphore_wait(barrier, len(peers))

    c = at["core"]
    copies = []
    for k in range(3):
        cp = pltpu.make_async_remote_copy(
            src_ref=x_ref.at[pl.ds(pl.multiple_of(k * COLOR_ROWS + (1 - c) * half, 8), half)],
            dst_ref=rcore.at[k], send_sem=core_send.at[k], recv_sem=core_recv.at[k],
            device_id=peer_of(at, "core", 1), device_id_type=MESH_IDS)
        cp.start()
        copies.append(cp)
    for k in range(3):
        copies[k].wait()
        base = k * COLOR_ROWS + c * half
        add_rows(lambda a, v, k=k: part.__setitem__((k, a), v),
                 lambda a, base=base: x_ref[pl.ds(pl.multiple_of(base, 8) + a.start, a.size)],
                 [lambda a, k=k: rcore[k, a]], half, 128)

    sources = (part, p1, p2)
    recvs = (r1, r2, r3)
    blocks = (COLOR_ROWS // 8, COLOR_ROWS // 32, COLOR_ROWS // 128)
    ranks = [[at[d] for d in order] for order in COLOR_ORDERS]
    for stage in range(3):
        blk = blocks[stage]
        src, rbuf = sources[stage], recvs[stage]
        staged = []
        for k, order in enumerate(COLOR_ORDERS):
            dim = order[stage]
            me = ranks[k][stage]
            row = []
            for s in (1, 2, 3):
                cp = pltpu.make_async_remote_copy(
                    src_ref=src.at[k, pl.ds(pl.multiple_of(((me + s) % 4) * blk, 8), blk)],
                    dst_ref=rbuf.at[k, s - 1], send_sem=rs_send.at[stage, k, s - 1],
                    recv_sem=rs_recv.at[stage, k, s - 1],
                    device_id=peer_of(at, dim, s), device_id_type=MESH_IDS)
                cp.start()
                row.append(cp)
            staged.append(row)
        for k in range(3):
            for cp in staged[k]:
                cp.wait()
            me = ranks[k][stage]
            own = pl.multiple_of(me * blk, 8)
            others = [lambda a, k=k, j=j: rbuf[k, j, a] for j in range(3)]
            first = lambda a, k=k, own=own, src=src: src[k, pl.ds(own + a.start, a.size)]
            if stage == 0:
                add_rows(lambda a, v, k=k: p1.__setitem__((k, a), v), first, others, blk, 128)
            elif stage == 1:
                add_rows(lambda a, v, k=k: p2.__setitem__((k, a), v), first, others, blk, blk)
            else:
                total = first(pl.ds(0, blk)) + others[0](pl.ds(0, blk)) + others[1](pl.ds(0, blk)) + others[2](pl.ds(0, blk))
                a, b, e = ranks[k]
                pos = pl.multiple_of(k * COLOR_ROWS + (c * 64 + a * 16 + b * 4 + e) * CHUNK_ROWS, 8)
                red[k] = total * scale
                lead = c * 64 + a * 16 + b * 4 + e
                put = pltpu.make_async_copy(
                    red.at[k], out_ref.at[pl.ds(jnp.minimum(pos, out_ref.shape[0] - blk), blk)], out_sem.at[k])

                @pl.when(real_chunk(k, lead))
                def _():
                    put.start()
                    put.wait()

    sizes = (COLOR_ROWS // 128, COLOR_ROWS // 32, COLOR_ROWS // 8)
    for step, stage in enumerate((2, 1, 0)):
        blk = sizes[step]
        staged = []
        for k, order in enumerate(COLOR_ORDERS):
            dim = order[stage]
            a, b, e = ranks[k]

            def lead_of(a, b, e):
                return (c * 64 + a * 16 + b * 4 + e, c * 64 + a * 16 + b * 4, c * 64 + a * 16)[step]

            lead = lead_of(a, b, e)
            pos = pl.multiple_of(k * COLOR_ROWS + lead * CHUNK_ROWS, 8)
            pos = jnp.minimum(pos, out_ref.shape[0] - blk)
            row = []
            for s in (1, 2, 3):
                moved = [a, b, e]
                moved[stage] = (moved[stage] + 4 - s) % 4
                cp = pltpu.make_async_remote_copy(
                    src_ref=out_ref.at[pl.ds(pos, blk)], dst_ref=out_ref.at[pl.ds(pos, blk)],
                    send_sem=ag_send.at[stage, k, s - 1], recv_sem=ag_recv.at[stage, k, s - 1],
                    device_id=peer_of(at, dim, s), device_id_type=MESH_IDS)
                mine, theirs = real_chunk(k, lead), real_chunk(k, lead_of(*moved))
                pl.when(mine)(cp.start)
                row.append((cp, mine, theirs))
            staged.append(row)
        for row in staged:
            for cp, mine, theirs in row:
                pl.when(mine)(cp.wait_send)
                pl.when(theirs)(cp.wait_recv)
    last = []
    for k in range(3):
        if k < 2:
            pos = pl.multiple_of(k * COLOR_ROWS + c * half, 8)
            size, mine, theirs = half, c >= 0, c >= 0
        else:
            pos = k * COLOR_ROWS
            size, mine, theirs = out_ref.shape[0] - pos, c == 0, c == 1
        cp = pltpu.make_async_remote_copy(
            src_ref=out_ref.at[pl.ds(pos, size)], dst_ref=out_ref.at[pl.ds(pos, size)],
            send_sem=agc_send.at[k], recv_sem=agc_recv.at[k],
            device_id=peer_of(at, "core", 1), device_id_type=MESH_IDS)
        pl.when(mine)(cp.start)
        last.append((cp, mine, theirs))
    for cp, mine, theirs in last:
        pl.when(mine)(cp.wait_send)
        pl.when(theirs)(cp.wait_recv)


def summed_everywhere(stacked, scale):
    rows = PAD_OFFSETS * 256
    width = stacked.shape[2]
    data = jnp.concatenate(
        [stacked, jnp.zeros((PAD_OFFSETS - stacked.shape[0],) + stacked.shape[1:], stacked.dtype)], 0
    ).reshape(rows, width)
    f32 = jnp.float32
    blocks = (COLOR_ROWS // 8, COLOR_ROWS // 32, COLOR_ROWS // 128)
    total = pl.pallas_call(
        functools.partial(allreduce_kernel, scale),
        out_shape=jax.ShapeDtypeStruct((REAL_ROWS, width), f32),
        in_specs=[pl.BlockSpec(memory_space=pltpu.VMEM)],
        out_specs=pl.BlockSpec(memory_space=pl.ANY),
        scratch_shapes=[
            pltpu.VMEM((3, COLOR_ROWS // 2, width), f32),
            pltpu.VMEM((3, COLOR_ROWS // 2, width), f32),
            pltpu.VMEM((3, 3, blocks[0], width), f32),
            pltpu.VMEM((3, blocks[0], width), f32),
            pltpu.VMEM((3, 3, blocks[1], width), f32),
            pltpu.VMEM((3, blocks[1], width), f32),
            pltpu.VMEM((3, 3, blocks[2], width), f32),
            pltpu.VMEM((3, blocks[2], width), f32),
            pltpu.SemaphoreType.DMA((3,)),
            pltpu.SemaphoreType.DMA((3,)),
            pltpu.SemaphoreType.DMA((3, 3, 3)),
            pltpu.SemaphoreType.DMA((3, 3, 3)),
            pltpu.SemaphoreType.DMA((3, 3, 3)),
            pltpu.SemaphoreType.DMA((3, 3, 3)),
            pltpu.SemaphoreType.DMA((3,)),
            pltpu.SemaphoreType.DMA((3,)),
            pltpu.SemaphoreType.DMA((3,)),
        ],
        compiler_params=pltpu.CompilerParams(
            collective_id=0, has_side_effects=True, vmem_limit_bytes=64 * 1024 * 1024
        ),
    )(data)
    return total.reshape(stacked.shape)


def passed_along(array, axis, by):
    peers = lax.axis_size(axis)
    pairs = [(i, i + by) for i in range(peers) if 0 <= i + by < peers]
    return lax.ppermute(array, axis, pairs)


def contract_rows(left, right):
    return lax.dot_general(
        left, right, (((0,), (0,)), ((), ())), preferred_element_type=jnp.float32
    )


def through_kernel(grads, kernel):
    return lax.dot_general(
        grads, kernel, (((1,), (1,)), ((), ())), preferred_element_type=jnp.float32
    )


def one_hot_rows(lists, rows_here):
    numbers = lax.broadcasted_iota(jnp.int32, lists.shape + (rows_here,), lists.ndim)
    return (lists[..., None] == numbers).astype(jnp.bfloat16)


def pick_rows(table, source):
    return jnp.einsum("...v,vc->...c", table, source, preferred_element_type=jnp.float32).astype(
        jnp.bfloat16
    )


def place_rows(table, rows):
    return jnp.einsum("fbv,fbc->vc", table, rows, preferred_element_type=jnp.float32)


def face_products(features, grads, kernels):
    weight_grad = jnp.einsum("fbc,fbd->fcd", features, grads, preferred_element_type=jnp.float32)
    out_rows = jnp.einsum(
        "fbd,fcd->fbc", grads, kernels, preferred_element_type=jnp.float32
    ).astype(jnp.bfloat16)
    return (weight_grad, out_rows)


def per_device(feats, grad_out, weight, loc_in, loc_out, bnd_out, bnd_in):
    rows_here = feats.shape[1]
    pairs = loc_in.shape[3]
    own_feat = feats[0]
    own_grad = grad_out[0]
    center = contract_rows(own_feat, own_grad)
    accumulated = through_kernel(own_grad, weight[13])
    table_in = one_hot_rows(loc_in[0, 0], rows_here)
    table_out = one_hot_rows(loc_out[0, 0], rows_here)
    gathered_x = pick_rows(table_in, own_feat)
    gathered_g = pick_rows(table_out, own_grad)
    placed = jnp.einsum(
        "kpv,kpc->vkc", table_in, gathered_g, preferred_element_type=jnp.float32
    ).astype(jnp.bfloat16)
    side_kernels = jnp.concatenate([weight[0:13], weight[14:27]], 0)
    accumulated = accumulated + jnp.einsum(
        "vkd,kcd->vc", placed, side_kernels, preferred_element_type=jnp.float32
    )
    offset_grads = jnp.einsum(
        "kpc,kpd->kcd", gathered_x, gathered_g, preferred_element_type=jnp.float32
    )
    low_kernels = weight[0:9]
    high_kernels = weight[18:27]
    face_out_table = one_hot_rows(bnd_out[0, 0], rows_here)
    face_in_table = one_hot_rows(bnd_in[0, 0], rows_here)
    own_grads = pick_rows(face_out_table, own_grad)
    asked = pick_rows(face_in_table, own_feat)
    from_below = passed_along(own_grads[1], "region", 1)
    from_above = passed_along(own_grads[0], "region", -1)
    high_grad, below_rows = face_products(asked[0], from_below, high_kernels)
    low_grad, above_rows = face_products(asked[1], from_above, low_kernels)
    accumulated = accumulated + place_rows(face_in_table[0], below_rows)
    accumulated = accumulated + place_rows(face_in_table[1], above_rows)
    stacked = jnp.concatenate(
        [
            offset_grads[0:9] + low_grad,
            offset_grads[9:13],
            center[None],
            offset_grads[13:17],
            offset_grads[17:26] + high_grad,
        ],
        0,
    )
    loss_scale = 1.0 / math.sqrt(pairs * lax.axis_size("dp") * lax.axis_size("region"))
    grad_weight = summed_everywhere(stacked, loss_scale)
    grad_input = accumulated.astype(jnp.bfloat16)[None]
    return (grad_input, grad_weight)


def solution(mesh):
    placed = (
        P("dp", "region", None),
        P("dp", "region", None),
        P(),
        P("dp", "region", None, None),
        P("dp", "region", None, None),
        P("dp", "region", None, None, None),
        P("dp", "region", None, None, None),
    )
    return jax.shard_map(
        per_device,
        mesh=mesh,
        in_specs=placed,
        out_specs=(P("dp", "region", None), P()),
        check_vma=False,
    )
```

```python
import functools
import math

import jax
import jax.numpy as jnp
from jax import lax
from jax.sharding import PartitionSpec as P

from jax.experimental import pallas as pl
from jax.experimental.pallas import tpu as pltpu

MESH_IDS = pl.DeviceIdType.MESH
COLOR_ORDERS = (("z", "y", "x"), ("y", "x", "z"), ("x", "z", "y"))
CHUNK_ROWS = 24
COLOR_ROWS = 128 * CHUNK_ROWS
PAD_OFFSETS = 36


def coords_here():
    r = lax.axis_index("region")
    return {"x": lax.axis_index("dp"), "y": r // 8, "z": (r // 2) % 4, "core": r % 2}


def peer_of(at, dim, shift):
    x, y, z, c = at["x"], at["y"], at["z"], at["core"]
    if dim == "x":
        x = (x + shift) % 4
    elif dim == "y":
        y = (y + shift) % 4
    elif dim == "z":
        z = (z + shift) % 4
    else:
        c = 1 - c
    return (x, (y * 4 + z) * 2 + c)


def add_rows(dst, first, others, rows, slab):
    def body(i, carry):
        at = pl.ds(pl.multiple_of(i * slab, slab), slab)
        total = first(at)
        for other in others:
            total = total + other(at)
        dst(at, total)
        return carry

    lax.fori_loop(0, rows // slab, body, 0)


def allreduce_kernel(scale, x_ref, out_ref, rcore, part, r1, p1, r2, p2, r3, red,
                     core_send, core_recv, rs_send, rs_recv, ag_send, ag_recv, agc_send, agc_recv, out_sem):
    at = coords_here()
    half = COLOR_ROWS // 2
    barrier = pltpu.get_barrier_semaphore()
    peers = [peer_of(at, "core", 1)] + [peer_of(at, d, s) for d in ("z", "y", "x") for s in (1, 2, 3)]
    for p in peers:
        pl.semaphore_signal(barrier, inc=1, device_id=p, device_id_type=MESH_IDS)
    pl.semaphore_wait(barrier, len(peers))

    c = at["core"]
    copies = []
    for k in range(3):
        cp = pltpu.make_async_remote_copy(
            src_ref=x_ref.at[pl.ds(pl.multiple_of(k * COLOR_ROWS + (1 - c) * half, 8), half)],
            dst_ref=rcore.at[k], send_sem=core_send.at[k], recv_sem=core_recv.at[k],
            device_id=peer_of(at, "core", 1), device_id_type=MESH_IDS)
        cp.start()
        copies.append(cp)
    sources = (part, p1, p2)
    recvs = (r1, r2, r3)
    blocks = (COLOR_ROWS // 8, COLOR_ROWS // 32, COLOR_ROWS // 128)
    ranks = [[at[d] for d in order] for order in COLOR_ORDERS]

    def scatter_sends(stage, k):
        blk, src, rbuf = blocks[stage], sources[stage], recvs[stage]
        dim, me = COLOR_ORDERS[k][stage], ranks[k][stage]
        row = []
        for s in (1, 2, 3):
            cp = pltpu.make_async_remote_copy(
                src_ref=src.at[k, pl.ds(pl.multiple_of(((me + s) % 4) * blk, 8), blk)],
                dst_ref=rbuf.at[k, s - 1], send_sem=rs_send.at[stage, k, s - 1],
                recv_sem=rs_recv.at[stage, k, s - 1],
                device_id=peer_of(at, dim, s), device_id_type=MESH_IDS)
            cp.start()
            row.append(cp)
        return row

    def gather_sends(step, k):
        stage = (2, 1, 0)[step]
        blk = (COLOR_ROWS // 128, COLOR_ROWS // 32, COLOR_ROWS // 8)[step]
        dim = COLOR_ORDERS[k][stage]
        a, b, e = ranks[k]
        lead = (c * 64 + a * 16 + b * 4 + e, c * 64 + a * 16 + b * 4, c * 64 + a * 16)[step]
        pos = pl.multiple_of(k * COLOR_ROWS + lead * CHUNK_ROWS, 8)
        row = []
        for s in (1, 2, 3):
            cp = pltpu.make_async_remote_copy(
                src_ref=out_ref.at[pl.ds(pos, blk)], dst_ref=out_ref.at[pl.ds(pos, blk)],
                send_sem=ag_send.at[stage, k, s - 1], recv_sem=ag_recv.at[stage, k, s - 1],
                device_id=peer_of(at, dim, s), device_id_type=MESH_IDS)
            cp.start()
            row.append(cp)
        return row

    def pair_send(k):
        pos = pl.multiple_of(k * COLOR_ROWS + c * half, 8)
        cp = pltpu.make_async_remote_copy(
            src_ref=out_ref.at[pl.ds(pos, half)], dst_ref=out_ref.at[pl.ds(pos, half)],
            send_sem=agc_send.at[k], recv_sem=agc_recv.at[k],
            device_id=peer_of(at, "core", 1), device_id_type=MESH_IDS)
        cp.start()
        return cp

    staged = [None] * 3
    for k in range(3):
        copies[k].wait()
        base = k * COLOR_ROWS + c * half
        add_rows(lambda a, v, k=k: part.__setitem__((k, a), v),
                 lambda a, base=base: x_ref[pl.ds(pl.multiple_of(base, 8) + a.start, a.size)],
                 [lambda a, k=k: rcore[k, a]], half, 128)
        staged[k] = scatter_sends(0, k)
    for stage in range(3):
        blk, src, rbuf = blocks[stage], sources[stage], recvs[stage]
        for k in range(3):
            for cp in staged[k]:
                cp.wait()
            me = ranks[k][stage]
            own = pl.multiple_of(me * blk, 8)
            others = [lambda a, k=k, j=j, rbuf=rbuf: rbuf[k, j, a] for j in range(3)]
            first = lambda a, k=k, own=own, src=src: src[k, pl.ds(own + a.start, a.size)]
            if stage == 0:
                add_rows(lambda a, v, k=k: p1.__setitem__((k, a), v), first, others, blk, 128)
                staged[k] = scatter_sends(1, k)
            elif stage == 1:
                add_rows(lambda a, v, k=k: p2.__setitem__((k, a), v), first, others, blk, blk)
                staged[k] = scatter_sends(2, k)
            else:
                total = first(pl.ds(0, blk)) + others[0](pl.ds(0, blk)) + others[1](pl.ds(0, blk)) + others[2](pl.ds(0, blk))
                a, b, e = ranks[k]
                pos = pl.multiple_of(k * COLOR_ROWS + (c * 64 + a * 16 + b * 4 + e) * CHUNK_ROWS, 8)
                red[k] = total * scale
                put = pltpu.make_async_copy(red.at[k], out_ref.at[pl.ds(pos, blk)], out_sem.at[k])
                put.start()
                put.wait()
                staged[k] = gather_sends(0, k)
    for step in range(3):
        for k in range(3):
            for cp in staged[k]:
                cp.wait()
            staged[k] = gather_sends(step + 1, k) if step < 2 else [pair_send(k)]
    for k in range(3):
        for cp in staged[k]:
            cp.wait()

def summed_everywhere(stacked, scale):
    rows = PAD_OFFSETS * 256
    width = stacked.shape[2]
    data = jnp.concatenate(
        [stacked, jnp.zeros((PAD_OFFSETS - stacked.shape[0],) + stacked.shape[1:], stacked.dtype)], 0
    ).reshape(rows, width)
    f32 = jnp.float32
    blocks = (COLOR_ROWS // 8, COLOR_ROWS // 32, COLOR_ROWS // 128)
    total = pl.pallas_call(
        functools.partial(allreduce_kernel, scale),
        out_shape=jax.ShapeDtypeStruct((rows, width), f32),
        in_specs=[pl.BlockSpec(memory_space=pltpu.VMEM)],
        out_specs=pl.BlockSpec(memory_space=pl.ANY),
        scratch_shapes=[
            pltpu.VMEM((3, COLOR_ROWS // 2, width), f32),
            pltpu.VMEM((3, COLOR_ROWS // 2, width), f32),
            pltpu.VMEM((3, 3, blocks[0], width), f32),
            pltpu.VMEM((3, blocks[0], width), f32),
            pltpu.VMEM((3, 3, blocks[1], width), f32),
            pltpu.VMEM((3, blocks[1], width), f32),
            pltpu.VMEM((3, 3, blocks[2], width), f32),
            pltpu.VMEM((3, blocks[2], width), f32),
            pltpu.SemaphoreType.DMA((3,)),
            pltpu.SemaphoreType.DMA((3,)),
            pltpu.SemaphoreType.DMA((3, 3, 3)),
            pltpu.SemaphoreType.DMA((3, 3, 3)),
            pltpu.SemaphoreType.DMA((3, 3, 3)),
            pltpu.SemaphoreType.DMA((3, 3, 3)),
            pltpu.SemaphoreType.DMA((3,)),
            pltpu.SemaphoreType.DMA((3,)),
            pltpu.SemaphoreType.DMA((3,)),
        ],
        compiler_params=pltpu.CompilerParams(
            collective_id=0, has_side_effects=True, vmem_limit_bytes=64 * 1024 * 1024
        ),
    )(data)
    return total[: stacked.shape[0] * stacked.shape[1]].reshape(stacked.shape)


def passed_along(array, axis, by):
    peers = lax.axis_size(axis)
    pairs = [(i, i + by) for i in range(peers) if 0 <= i + by < peers]
    return lax.ppermute(array, axis, pairs)


def contract_rows(left, right):
    return lax.dot_general(
        left, right, (((0,), (0,)), ((), ())), preferred_element_type=jnp.float32
    )


def through_kernel(grads, kernel):
    return lax.dot_general(
        grads, kernel, (((1,), (1,)), ((), ())), preferred_element_type=jnp.float32
    )


def one_hot_rows(lists, rows_here):
    numbers = lax.broadcasted_iota(jnp.int32, lists.shape + (rows_here,), lists.ndim)
    return (lists[..., None] == numbers).astype(jnp.bfloat16)


def pick_rows(table, source):
    return jnp.einsum("...v,vc->...c", table, source, preferred_element_type=jnp.float32).astype(
        jnp.bfloat16
    )


def place_rows(table, rows):
    return jnp.einsum("fbv,fbc->vc", table, rows, preferred_element_type=jnp.float32)


def face_products(features, grads, kernels):
    weight_grad = jnp.einsum("fbc,fbd->fcd", features, grads, preferred_element_type=jnp.float32)
    out_rows = jnp.einsum(
        "fbd,fcd->fbc", grads, kernels, preferred_element_type=jnp.float32
    ).astype(jnp.bfloat16)
    return (weight_grad, out_rows)


def per_device(feats, grad_out, weight, loc_in, loc_out, bnd_out, bnd_in):
    rows_here = feats.shape[1]
    pairs = loc_in.shape[3]
    own_feat = feats[0]
    own_grad = grad_out[0]
    center = contract_rows(own_feat, own_grad)
    accumulated = through_kernel(own_grad, weight[13])
    table_in = one_hot_rows(loc_in[0, 0], rows_here)
    table_out = one_hot_rows(loc_out[0, 0], rows_here)
    gathered_x = pick_rows(table_in, own_feat)
    gathered_g = pick_rows(table_out, own_grad)
    placed = jnp.einsum(
        "kpv,kpc->vkc", table_in, gathered_g, preferred_element_type=jnp.float32
    ).astype(jnp.bfloat16)
    side_kernels = jnp.concatenate([weight[0:13], weight[14:27]], 0)
    accumulated = accumulated + jnp.einsum(
        "vkd,kcd->vc", placed, side_kernels, preferred_element_type=jnp.float32
    )
    offset_grads = jnp.einsum(
        "kpc,kpd->kcd", gathered_x, gathered_g, preferred_element_type=jnp.float32
    )
    low_kernels = weight[0:9]
    high_kernels = weight[18:27]
    face_out_table = one_hot_rows(bnd_out[0, 0], rows_here)
    face_in_table = one_hot_rows(bnd_in[0, 0], rows_here)
    own_grads = pick_rows(face_out_table, own_grad)
    asked = pick_rows(face_in_table, own_feat)
    from_below = passed_along(own_grads[1], "region", 1)
    from_above = passed_along(own_grads[0], "region", -1)
    high_grad, below_rows = face_products(asked[0], from_below, high_kernels)
    low_grad, above_rows = face_products(asked[1], from_above, low_kernels)
    accumulated = accumulated + place_rows(face_in_table[0], below_rows)
    accumulated = accumulated + place_rows(face_in_table[1], above_rows)
    stacked = jnp.concatenate(
        [
            offset_grads[0:9] + low_grad,
            offset_grads[9:13],
            center[None],
            offset_grads[13:17],
            offset_grads[17:26] + high_grad,
        ],
        0,
    )
    loss_scale = 1.0 / math.sqrt(pairs * lax.axis_size("dp") * lax.axis_size("region"))
    grad_weight = summed_everywhere(stacked, loss_scale)
    grad_input = accumulated.astype(jnp.bfloat16)[None]
    return (grad_input, grad_weight)


def solution(mesh):
    placed = (
        P("dp", "region", None),
        P("dp", "region", None),
        P(),
        P("dp", "region", None, None),
        P("dp", "region", None, None),
        P("dp", "region", None, None, None),
        P("dp", "region", None, None, None),
    )
    return jax.shard_map(
        per_device,
        mesh=mesh,
        in_specs=placed,
        out_specs=(P("dp", "region", None), P()),
        check_vma=False,
    )
```

```python
import functools
import math

import jax
import jax.numpy as jnp
from jax import lax
from jax.sharding import PartitionSpec as P

from jax.experimental import pallas as pl
from jax.experimental.pallas import tpu as pltpu

MESH_IDS = pl.DeviceIdType.MESH
COLOR_ORDERS = (("z", "y", "x"), ("y", "x", "z"), ("x", "z", "y"))
CHUNK_ROWS = 24
COLOR_ROWS = 128 * CHUNK_ROWS
PAD_OFFSETS = 36


def coords_here():
    r = lax.axis_index("region")
    return {"x": lax.axis_index("dp"), "y": r // 8, "z": (r // 2) % 4, "core": r % 2}


def peer_of(at, dim, shift):
    x, y, z, c = at["x"], at["y"], at["z"], at["core"]
    if dim == "x":
        x = (x + shift) % 4
    elif dim == "y":
        y = (y + shift) % 4
    elif dim == "z":
        z = (z + shift) % 4
    else:
        c = 1 - c
    return (x, (y * 4 + z) * 2 + c)


def add_rows(dst, first, others, rows, slab):
    def body(i, carry):
        at = pl.ds(pl.multiple_of(i * slab, slab), slab)
        total = first(at)
        for other in others:
            total = total + other(at)
        dst(at, total)
        return carry

    lax.fori_loop(0, rows // slab, body, 0)


def allreduce_kernel(scale, x_ref, out_ref, rcore, part, rr0, sb0, p1, rr1, sb1, p2, r3, red,
                     core_send, core_recv, rs_send, rs_recv, ag_send, ag_recv, agc_send, agc_recv, out_sem,
                     ring_send, ring_recv, ring_ag_send, ring_ag_recv):
    at = coords_here()
    half = COLOR_ROWS // 2
    barrier = pltpu.get_barrier_semaphore()
    peers = [peer_of(at, "core", 1)] + [peer_of(at, d, s) for d in ("z", "y", "x") for s in (1, 2, 3)]
    for p in peers:
        pl.semaphore_signal(barrier, inc=1, device_id=p, device_id_type=MESH_IDS)
    pl.semaphore_wait(barrier, len(peers))

    c = at["core"]
    copies = []
    for k in range(3):
        cp = pltpu.make_async_remote_copy(
            src_ref=x_ref.at[pl.ds(pl.multiple_of(k * COLOR_ROWS + (1 - c) * half, 8), half)],
            dst_ref=rcore.at[k], send_sem=core_send.at[k], recv_sem=core_recv.at[k],
            device_id=peer_of(at, "core", 1), device_id_type=MESH_IDS)
        cp.start()
        copies.append(cp)
    sources = (part, p1, p2)
    recvs = (None, None, r3)
    blocks = (COLOR_ROWS // 8, COLOR_ROWS // 32, COLOR_ROWS // 128)
    ranks = [[at[d] for d in order] for order in COLOR_ORDERS]

    def scatter_sends(stage, k):
        blk, src, rbuf = blocks[stage], sources[stage], recvs[stage]
        dim, me = COLOR_ORDERS[k][stage], ranks[k][stage]
        row = []
        for s in (1, 2, 3):
            cp = pltpu.make_async_remote_copy(
                src_ref=src.at[k, pl.ds(pl.multiple_of(((me + s) % 4) * blk, 8), blk)],
                dst_ref=rbuf.at[k, s - 1], send_sem=rs_send.at[stage, k, s - 1],
                recv_sem=rs_recv.at[stage, k, s - 1],
                device_id=peer_of(at, dim, s), device_id_type=MESH_IDS)
            cp.start()
            row.append(cp)
        return row

    def gather_sends(step, k):
        stage = (2, 1, 0)[step]
        blk = (COLOR_ROWS // 128, COLOR_ROWS // 32, COLOR_ROWS // 8)[step]
        dim = COLOR_ORDERS[k][stage]
        a, b, e = ranks[k]
        lead = (c * 64 + a * 16 + b * 4 + e, c * 64 + a * 16 + b * 4, c * 64 + a * 16)[step]
        pos = pl.multiple_of(k * COLOR_ROWS + lead * CHUNK_ROWS, 8)
        row = []
        for s in (1, 2, 3):
            cp = pltpu.make_async_remote_copy(
                src_ref=out_ref.at[pl.ds(pos, blk)], dst_ref=out_ref.at[pl.ds(pos, blk)],
                send_sem=ag_send.at[stage, k, s - 1], recv_sem=ag_recv.at[stage, k, s - 1],
                device_id=peer_of(at, dim, s), device_id_type=MESH_IDS)
            cp.start()
            row.append(cp)
        return row

    def pair_send(k):
        pos = pl.multiple_of(k * COLOR_ROWS + c * half, 8)
        cp = pltpu.make_async_remote_copy(
            src_ref=out_ref.at[pl.ds(pos, half)], dst_ref=out_ref.at[pl.ds(pos, half)],
            send_sem=agc_send.at[k], recv_sem=agc_recv.at[k],
            device_id=peer_of(at, "core", 1), device_id_type=MESH_IDS)
        cp.start()
        return cp

    rings = ((rr0, sb0), (rr1, sb1))
    nexts = (p1, p2)

    def own_half(stage, k, chunk, d):
        blk = blocks[stage]
        return sources[stage].at[k, pl.ds(pl.multiple_of(chunk * blk + d * (blk // 2), 8), blk // 2)]

    def ring_peer(stage, k, d):
        return peer_of(at, COLOR_ORDERS[k][stage], 1 if d == 0 else 3)

    def scatter_ring(stage):
        rr, sb = rings[stage]
        live = {}
        for k in range(3):
            me = ranks[k][stage]
            for d in range(2):
                chunk = (me + 3) % 4 if d == 0 else (me + 1) % 4
                cp = pltpu.make_async_remote_copy(
                    src_ref=own_half(stage, k, chunk, d), dst_ref=rr.at[k, d, 0],
                    send_sem=ring_send.at[stage, k, d, 0], recv_sem=ring_recv.at[stage, k, d, 0],
                    device_id=ring_peer(stage, k, d), device_id_type=MESH_IDS)
                cp.start()
                live[k, d] = cp
        for t in (1, 2):
            for k in range(3):
                me = ranks[k][stage]
                for d in range(2):
                    live[k, d].wait()
                    chunk = (me + 3 - t) % 4 if d == 0 else (me + t + 1) % 4
                    sb[k, d, t] = rr[k, d, t - 1] + own_half(stage, k, chunk, d)[...]
                    cp = pltpu.make_async_remote_copy(
                        src_ref=sb.at[k, d, t], dst_ref=rr.at[k, d, t],
                        send_sem=ring_send.at[stage, k, d, t], recv_sem=ring_recv.at[stage, k, d, t],
                        device_id=ring_peer(stage, k, d), device_id_type=MESH_IDS)
                    cp.start()
                    live[k, d] = cp
        for k in range(3):
            me = ranks[k][stage]
            h = blocks[stage] // 2
            for d in range(2):
                live[k, d].wait()
                nexts[stage][k, pl.ds(d * h, h)] = rr[k, d, 2] + own_half(stage, k, me, d)[...]

    def gather_ring(stage):
        blk = blocks[stage]
        h = blk // 2
        live = {}
        for t in range(3):
            for k in range(3):
                a, b, e = ranks[k]
                me = ranks[k][stage]
                parent = (c * 64, c * 64 + a * 16)[stage]
                for d in range(2):
                    if t > 0:
                        live[k, d].wait()
                    chunk = (me + 4 - t) % 4 if d == 0 else (me + t) % 4
                    pos = pl.multiple_of(k * COLOR_ROWS + parent * CHUNK_ROWS + chunk * blk + d * h, 8)
                    cp = pltpu.make_async_remote_copy(
                        src_ref=out_ref.at[pl.ds(pos, h)], dst_ref=out_ref.at[pl.ds(pos, h)],
                        send_sem=ring_ag_send.at[stage, k, d, t], recv_sem=ring_ag_recv.at[stage, k, d, t],
                        device_id=ring_peer(stage, k, d), device_id_type=MESH_IDS)
                    cp.start()
                    live[k, d] = cp
        for k in range(3):
            for d in range(2):
                live[k, d].wait()

    for k in range(3):
        copies[k].wait()
        base = k * COLOR_ROWS + c * half
        add_rows(lambda a, v, k=k: part.__setitem__((k, a), v),
                 lambda a, base=base: x_ref[pl.ds(pl.multiple_of(base, 8) + a.start, a.size)],
                 [lambda a, k=k: rcore[k, a]], half, 128)
    scatter_ring(0)
    scatter_ring(1)
    staged = [scatter_sends(2, k) for k in range(3)]
    blk = blocks[2]
    for k in range(3):
        for cp in staged[k]:
            cp.wait()
        me = ranks[k][2]
        own = pl.multiple_of(me * blk, 8)
        total = p2[k, pl.ds(own, blk)] + r3[k, 0] + r3[k, 1] + r3[k, 2]
        a, b, e = ranks[k]
        pos = pl.multiple_of(k * COLOR_ROWS + (c * 64 + a * 16 + b * 4 + e) * CHUNK_ROWS, 8)
        red[k] = total * scale
        put = pltpu.make_async_copy(red.at[k], out_ref.at[pl.ds(pos, blk)], out_sem.at[k])
        put.start()
        put.wait()
        staged[k] = gather_sends(0, k)
    for k in range(3):
        for cp in staged[k]:
            cp.wait()
    gather_ring(1)
    gather_ring(0)
    staged = [[pair_send(k)] for k in range(3)]
    for k in range(3):
        for cp in staged[k]:
            cp.wait()

def summed_everywhere(stacked, scale):
    rows = PAD_OFFSETS * 256
    width = stacked.shape[2]
    data = jnp.concatenate(
        [stacked, jnp.zeros((PAD_OFFSETS - stacked.shape[0],) + stacked.shape[1:], stacked.dtype)], 0
    ).reshape(rows, width)
    f32 = jnp.float32
    blocks = (COLOR_ROWS // 8, COLOR_ROWS // 32, COLOR_ROWS // 128)
    total = pl.pallas_call(
        functools.partial(allreduce_kernel, scale),
        out_shape=jax.ShapeDtypeStruct((rows, width), f32),
        in_specs=[pl.BlockSpec(memory_space=pltpu.VMEM)],
        out_specs=pl.BlockSpec(memory_space=pl.ANY),
        scratch_shapes=[
            pltpu.VMEM((3, COLOR_ROWS // 2, width), f32),
            pltpu.VMEM((3, COLOR_ROWS // 2, width), f32),
            pltpu.VMEM((3, 2, 3, blocks[0] // 2, width), f32),
            pltpu.VMEM((3, 2, 3, blocks[0] // 2, width), f32),
            pltpu.VMEM((3, blocks[0], width), f32),
            pltpu.VMEM((3, 2, 3, blocks[1] // 2, width), f32),
            pltpu.VMEM((3, 2, 3, blocks[1] // 2, width), f32),
            pltpu.VMEM((3, blocks[1], width), f32),
            pltpu.VMEM((3, 3, blocks[2], width), f32),
            pltpu.VMEM((3, blocks[2], width), f32),
            pltpu.SemaphoreType.DMA((3,)),
            pltpu.SemaphoreType.DMA((3,)),
            pltpu.SemaphoreType.DMA((3, 3, 3)),
            pltpu.SemaphoreType.DMA((3, 3, 3)),
            pltpu.SemaphoreType.DMA((3, 3, 3)),
            pltpu.SemaphoreType.DMA((3, 3, 3)),
            pltpu.SemaphoreType.DMA((3,)),
            pltpu.SemaphoreType.DMA((3,)),
            pltpu.SemaphoreType.DMA((3,)),
            pltpu.SemaphoreType.DMA((2, 3, 2, 3)),
            pltpu.SemaphoreType.DMA((2, 3, 2, 3)),
            pltpu.SemaphoreType.DMA((2, 3, 2, 3)),
            pltpu.SemaphoreType.DMA((2, 3, 2, 3)),
        ],
        compiler_params=pltpu.CompilerParams(
            collective_id=0, has_side_effects=True, vmem_limit_bytes=64 * 1024 * 1024
        ),
    )(data)
    return total[: stacked.shape[0] * stacked.shape[1]].reshape(stacked.shape)


def passed_along(array, axis, by):
    peers = lax.axis_size(axis)
    pairs = [(i, i + by) for i in range(peers) if 0 <= i + by < peers]
    return lax.ppermute(array, axis, pairs)


def contract_rows(left, right):
    return lax.dot_general(
        left, right, (((0,), (0,)), ((), ())), preferred_element_type=jnp.float32
    )


def through_kernel(grads, kernel):
    return lax.dot_general(
        grads, kernel, (((1,), (1,)), ((), ())), preferred_element_type=jnp.float32
    )


def one_hot_rows(lists, rows_here):
    numbers = lax.broadcasted_iota(jnp.int32, lists.shape + (rows_here,), lists.ndim)
    return (lists[..., None] == numbers).astype(jnp.bfloat16)


def pick_rows(table, source):
    return jnp.einsum("...v,vc->...c", table, source, preferred_element_type=jnp.float32).astype(
        jnp.bfloat16
    )


def place_rows(table, rows):
    return jnp.einsum("fbv,fbc->vc", table, rows, preferred_element_type=jnp.float32)


def face_products(features, grads, kernels):
    weight_grad = jnp.einsum("fbc,fbd->fcd", features, grads, preferred_element_type=jnp.float32)
    out_rows = jnp.einsum(
        "fbd,fcd->fbc", grads, kernels, preferred_element_type=jnp.float32
    ).astype(jnp.bfloat16)
    return (weight_grad, out_rows)


def per_device(feats, grad_out, weight, loc_in, loc_out, bnd_out, bnd_in):
    rows_here = feats.shape[1]
    pairs = loc_in.shape[3]
    own_feat = feats[0]
    own_grad = grad_out[0]
    center = contract_rows(own_feat, own_grad)
    accumulated = through_kernel(own_grad, weight[13])
    table_in = one_hot_rows(loc_in[0, 0], rows_here)
    table_out = one_hot_rows(loc_out[0, 0], rows_here)
    gathered_x = pick_rows(table_in, own_feat)
    gathered_g = pick_rows(table_out, own_grad)
    placed = jnp.einsum(
        "kpv,kpc->vkc", table_in, gathered_g, preferred_element_type=jnp.float32
    ).astype(jnp.bfloat16)
    side_kernels = jnp.concatenate([weight[0:13], weight[14:27]], 0)
    accumulated = accumulated + jnp.einsum(
        "vkd,kcd->vc", placed, side_kernels, preferred_element_type=jnp.float32
    )
    offset_grads = jnp.einsum(
        "kpc,kpd->kcd", gathered_x, gathered_g, preferred_element_type=jnp.float32
    )
    low_kernels = weight[0:9]
    high_kernels = weight[18:27]
    face_out_table = one_hot_rows(bnd_out[0, 0], rows_here)
    face_in_table = one_hot_rows(bnd_in[0, 0], rows_here)
    own_grads = pick_rows(face_out_table, own_grad)
    asked = pick_rows(face_in_table, own_feat)
    from_below = passed_along(own_grads[1], "region", 1)
    from_above = passed_along(own_grads[0], "region", -1)
    high_grad, below_rows = face_products(asked[0], from_below, high_kernels)
    low_grad, above_rows = face_products(asked[1], from_above, low_kernels)
    accumulated = accumulated + place_rows(face_in_table[0], below_rows)
    accumulated = accumulated + place_rows(face_in_table[1], above_rows)
    stacked = jnp.concatenate(
        [
            offset_grads[0:9] + low_grad,
            offset_grads[9:13],
            center[None],
            offset_grads[13:17],
            offset_grads[17:26] + high_grad,
        ],
        0,
    )
    loss_scale = 1.0 / math.sqrt(pairs * lax.axis_size("dp") * lax.axis_size("region"))
    grad_weight = summed_everywhere(stacked, loss_scale)
    grad_input = accumulated.astype(jnp.bfloat16)[None]
    return (grad_input, grad_weight)


def solution(mesh):
    placed = (
        P("dp", "region", None),
        P("dp", "region", None),
        P(),
        P("dp", "region", None, None),
        P("dp", "region", None, None),
        P("dp", "region", None, None, None),
        P("dp", "region", None, None, None),
    )
    return jax.shard_map(
        per_device,
        mesh=mesh,
        in_specs=placed,
        out_specs=(P("dp", "region", None), P()),
        check_vma=False,
    )
```

```python
import functools
import math

import jax
import jax.numpy as jnp
from jax import lax
from jax.sharding import PartitionSpec as P

from jax.experimental import pallas as pl
from jax.experimental.pallas import tpu as pltpu

MESH_IDS = pl.DeviceIdType.MESH
COLOR_ORDERS = (("z", "y", "x"), ("y", "x", "z"), ("x", "z", "y"))
CHUNK_ROWS = 24
COLOR_ROWS = 128 * CHUNK_ROWS
PAD_OFFSETS = 36


def coords_here():
    r = lax.axis_index("region")
    return {"x": lax.axis_index("dp"), "y": r // 8, "z": (r // 2) % 4, "core": r % 2}


def peer_of(at, dim, shift):
    x, y, z, c = at["x"], at["y"], at["z"], at["core"]
    if dim == "x":
        x = (x + shift) % 4
    elif dim == "y":
        y = (y + shift) % 4
    elif dim == "z":
        z = (z + shift) % 4
    else:
        c = 1 - c
    return (x, (y * 4 + z) * 2 + c)


def add_rows(dst, first, others, rows, slab):
    def body(i, carry):
        at = pl.ds(pl.multiple_of(i * slab, slab), slab)
        total = first(at)
        for other in others:
            total = total + other(at)
        dst(at, total)
        return carry

    lax.fori_loop(0, rows // slab, body, 0)


def allreduce_kernel(scale, x_ref, placed_ref, kmat_ref, out_ref, side_ref, rcore, part, r1, p1, r2, p2, r3, red,
                     core_send, core_recv, rs_send, rs_recv, ag_send, ag_recv, agc_send, agc_recv, out_sem):
    at = coords_here()
    half = COLOR_ROWS // 2

    def side_part(j0, j1):
        for j in range(j0, j1):
            term = jnp.dot(placed_ref[:, j * 256:(j + 1) * 256], kmat_ref[j * 256:(j + 1) * 256, :],
                           preferred_element_type=jnp.float32)
            if j == 0:
                side_ref[...] = term
            else:
                side_ref[...] += term
    barrier = pltpu.get_barrier_semaphore()
    peers = [peer_of(at, "core", 1)] + [peer_of(at, d, s) for d in ("z", "y", "x") for s in (1, 2, 3)]
    for p in peers:
        pl.semaphore_signal(barrier, inc=1, device_id=p, device_id_type=MESH_IDS)
    pl.semaphore_wait(barrier, len(peers))

    c = at["core"]
    copies = []
    for k in range(3):
        cp = pltpu.make_async_remote_copy(
            src_ref=x_ref.at[pl.ds(pl.multiple_of(k * COLOR_ROWS + (1 - c) * half, 8), half)],
            dst_ref=rcore.at[k], send_sem=core_send.at[k], recv_sem=core_recv.at[k],
            device_id=peer_of(at, "core", 1), device_id_type=MESH_IDS)
        cp.start()
        copies.append(cp)
    side_part(0, 4)
    sources = (part, p1, p2)
    recvs = (r1, r2, r3)
    blocks = (COLOR_ROWS // 8, COLOR_ROWS // 32, COLOR_ROWS // 128)
    ranks = [[at[d] for d in order] for order in COLOR_ORDERS]

    def scatter_sends(stage, k):
        blk, src, rbuf = blocks[stage], sources[stage], recvs[stage]
        dim, me = COLOR_ORDERS[k][stage], ranks[k][stage]
        row = []
        for s in (1, 2, 3):
            cp = pltpu.make_async_remote_copy(
                src_ref=src.at[k, pl.ds(pl.multiple_of(((me + s) % 4) * blk, 8), blk)],
                dst_ref=rbuf.at[k, s - 1], send_sem=rs_send.at[stage, k, s - 1],
                recv_sem=rs_recv.at[stage, k, s - 1],
                device_id=peer_of(at, dim, s), device_id_type=MESH_IDS)
            cp.start()
            row.append(cp)
        return row

    def gather_sends(step, k):
        stage = (2, 1, 0)[step]
        blk = (COLOR_ROWS // 128, COLOR_ROWS // 32, COLOR_ROWS // 8)[step]
        dim = COLOR_ORDERS[k][stage]
        a, b, e = ranks[k]
        lead = (c * 64 + a * 16 + b * 4 + e, c * 64 + a * 16 + b * 4, c * 64 + a * 16)[step]
        pos = pl.multiple_of(k * COLOR_ROWS + lead * CHUNK_ROWS, 8)
        row = []
        for s in (1, 2, 3):
            cp = pltpu.make_async_remote_copy(
                src_ref=out_ref.at[pl.ds(pos, blk)], dst_ref=out_ref.at[pl.ds(pos, blk)],
                send_sem=ag_send.at[stage, k, s - 1], recv_sem=ag_recv.at[stage, k, s - 1],
                device_id=peer_of(at, dim, s), device_id_type=MESH_IDS)
            cp.start()
            row.append(cp)
        return row

    def pair_send(k):
        pos = pl.multiple_of(k * COLOR_ROWS + c * half, 8)
        cp = pltpu.make_async_remote_copy(
            src_ref=out_ref.at[pl.ds(pos, half)], dst_ref=out_ref.at[pl.ds(pos, half)],
            send_sem=agc_send.at[k], recv_sem=agc_recv.at[k],
            device_id=peer_of(at, "core", 1), device_id_type=MESH_IDS)
        cp.start()
        return cp

    staged = [None] * 3
    for k in range(3):
        copies[k].wait()
        base = k * COLOR_ROWS + c * half
        add_rows(lambda a, v, k=k: part.__setitem__((k, a), v),
                 lambda a, base=base: x_ref[pl.ds(pl.multiple_of(base, 8) + a.start, a.size)],
                 [lambda a, k=k: rcore[k, a]], half, 128)
        staged[k] = scatter_sends(0, k)
    for stage in range(3):
        blk, src, rbuf = blocks[stage], sources[stage], recvs[stage]
        side_part(4 + 4 * stage, 8 + 4 * stage)
        for k in range(3):
            for cp in staged[k]:
                cp.wait()
            me = ranks[k][stage]
            own = pl.multiple_of(me * blk, 8)
            others = [lambda a, k=k, j=j, rbuf=rbuf: rbuf[k, j, a] for j in range(3)]
            first = lambda a, k=k, own=own, src=src: src[k, pl.ds(own + a.start, a.size)]
            if stage == 0:
                add_rows(lambda a, v, k=k: p1.__setitem__((k, a), v), first, others, blk, 128)
                staged[k] = scatter_sends(1, k)
            elif stage == 1:
                add_rows(lambda a, v, k=k: p2.__setitem__((k, a), v), first, others, blk, blk)
                staged[k] = scatter_sends(2, k)
            else:
                total = first(pl.ds(0, blk)) + others[0](pl.ds(0, blk)) + others[1](pl.ds(0, blk)) + others[2](pl.ds(0, blk))
                a, b, e = ranks[k]
                pos = pl.multiple_of(k * COLOR_ROWS + (c * 64 + a * 16 + b * 4 + e) * CHUNK_ROWS, 8)
                red[k] = total * scale
                put = pltpu.make_async_copy(red.at[k], out_ref.at[pl.ds(pos, blk)], out_sem.at[k])
                put.start()
                put.wait()
                staged[k] = gather_sends(0, k)
    for step in range(3):
        side_part(16 + 3 * step, 19 + 3 * step)
        for k in range(3):
            for cp in staged[k]:
                cp.wait()
            staged[k] = gather_sends(step + 1, k) if step < 2 else [pair_send(k)]
    side_part(25, 26)
    for k in range(3):
        for cp in staged[k]:
            cp.wait()

def summed_everywhere(stacked, scale, placed, kmat):
    rows = PAD_OFFSETS * 256
    width = stacked.shape[2]
    data = jnp.concatenate(
        [stacked, jnp.zeros((PAD_OFFSETS - stacked.shape[0],) + stacked.shape[1:], stacked.dtype)], 0
    ).reshape(rows, width)
    f32 = jnp.float32
    blocks = (COLOR_ROWS // 8, COLOR_ROWS // 32, COLOR_ROWS // 128)
    total, side = pl.pallas_call(
        functools.partial(allreduce_kernel, scale),
        out_shape=(jax.ShapeDtypeStruct((rows, width), f32),
                   jax.ShapeDtypeStruct((placed.shape[0], kmat.shape[1]), f32)),
        in_specs=[pl.BlockSpec(memory_space=pltpu.VMEM)] * 3,
        out_specs=(pl.BlockSpec(memory_space=pl.ANY), pl.BlockSpec(memory_space=pltpu.VMEM)),
        scratch_shapes=[
            pltpu.VMEM((3, COLOR_ROWS // 2, width), f32),
            pltpu.VMEM((3, COLOR_ROWS // 2, width), f32),
            pltpu.VMEM((3, 3, blocks[0], width), f32),
            pltpu.VMEM((3, blocks[0], width), f32),
            pltpu.VMEM((3, 3, blocks[1], width), f32),
            pltpu.VMEM((3, blocks[1], width), f32),
            pltpu.VMEM((3, 3, blocks[2], width), f32),
            pltpu.VMEM((3, blocks[2], width), f32),
            pltpu.SemaphoreType.DMA((3,)),
            pltpu.SemaphoreType.DMA((3,)),
            pltpu.SemaphoreType.DMA((3, 3, 3)),
            pltpu.SemaphoreType.DMA((3, 3, 3)),
            pltpu.SemaphoreType.DMA((3, 3, 3)),
            pltpu.SemaphoreType.DMA((3, 3, 3)),
            pltpu.SemaphoreType.DMA((3,)),
            pltpu.SemaphoreType.DMA((3,)),
            pltpu.SemaphoreType.DMA((3,)),
        ],
        compiler_params=pltpu.CompilerParams(
            collective_id=0, has_side_effects=True, vmem_limit_bytes=64 * 1024 * 1024
        ),
    )(data, placed, kmat)
    return total[: stacked.shape[0] * stacked.shape[1]].reshape(stacked.shape), side


def passed_along(array, axis, by):
    peers = lax.axis_size(axis)
    pairs = [(i, i + by) for i in range(peers) if 0 <= i + by < peers]
    return lax.ppermute(array, axis, pairs)


def contract_rows(left, right):
    return lax.dot_general(
        left, right, (((0,), (0,)), ((), ())), preferred_element_type=jnp.float32
    )


def through_kernel(grads, kernel):
    return lax.dot_general(
        grads, kernel, (((1,), (1,)), ((), ())), preferred_element_type=jnp.float32
    )


def one_hot_rows(lists, rows_here):
    numbers = lax.broadcasted_iota(jnp.int32, lists.shape + (rows_here,), lists.ndim)
    return (lists[..., None] == numbers).astype(jnp.bfloat16)


def pick_rows(table, source):
    return jnp.einsum("...v,vc->...c", table, source, preferred_element_type=jnp.float32).astype(
        jnp.bfloat16
    )


def place_rows(table, rows):
    return jnp.einsum("fbv,fbc->vc", table, rows, preferred_element_type=jnp.float32)


def face_products(features, grads, kernels):
    weight_grad = jnp.einsum("fbc,fbd->fcd", features, grads, preferred_element_type=jnp.float32)
    out_rows = jnp.einsum(
        "fbd,fcd->fbc", grads, kernels, preferred_element_type=jnp.float32
    ).astype(jnp.bfloat16)
    return (weight_grad, out_rows)


def per_device(feats, grad_out, weight, loc_in, loc_out, bnd_out, bnd_in):
    rows_here = feats.shape[1]
    pairs = loc_in.shape[3]
    own_feat = feats[0]
    own_grad = grad_out[0]
    center = contract_rows(own_feat, own_grad)
    accumulated = through_kernel(own_grad, weight[13])
    table_in = one_hot_rows(loc_in[0, 0], rows_here)
    table_out = one_hot_rows(loc_out[0, 0], rows_here)
    gathered_x = pick_rows(table_in, own_feat)
    gathered_g = pick_rows(table_out, own_grad)
    placed = jnp.einsum(
        "kpv,kpc->vkc", table_in, gathered_g, preferred_element_type=jnp.float32
    ).astype(jnp.bfloat16)
    side_kernels = jnp.concatenate([weight[0:13], weight[14:27]], 0)
    kmat = jnp.swapaxes(side_kernels, 1, 2).reshape(-1, side_kernels.shape[1])
    placed = placed.reshape(placed.shape[0], -1)
    offset_grads = jnp.einsum(
        "kpc,kpd->kcd", gathered_x, gathered_g, preferred_element_type=jnp.float32
    )
    low_kernels = weight[0:9]
    high_kernels = weight[18:27]
    face_out_table = one_hot_rows(bnd_out[0, 0], rows_here)
    face_in_table = one_hot_rows(bnd_in[0, 0], rows_here)
    own_grads = pick_rows(face_out_table, own_grad)
    asked = pick_rows(face_in_table, own_feat)
    from_below = passed_along(own_grads[1], "region", 1)
    from_above = passed_along(own_grads[0], "region", -1)
    high_grad, below_rows = face_products(asked[0], from_below, high_kernels)
    low_grad, above_rows = face_products(asked[1], from_above, low_kernels)
    accumulated = accumulated + place_rows(face_in_table[0], below_rows)
    accumulated = accumulated + place_rows(face_in_table[1], above_rows)
    stacked = jnp.concatenate(
        [
            offset_grads[0:9] + low_grad,
            offset_grads[9:13],
            center[None],
            offset_grads[13:17],
            offset_grads[17:26] + high_grad,
        ],
        0,
    )
    loss_scale = 1.0 / math.sqrt(pairs * lax.axis_size("dp") * lax.axis_size("region"))
    grad_weight, side = summed_everywhere(stacked, loss_scale, placed, kmat)
    accumulated = accumulated + side
    grad_input = accumulated.astype(jnp.bfloat16)[None]
    return (grad_input, grad_weight)


def solution(mesh):
    placed = (
        P("dp", "region", None),
        P("dp", "region", None),
        P(),
        P("dp", "region", None, None),
        P("dp", "region", None, None),
        P("dp", "region", None, None, None),
        P("dp", "region", None, None, None),
    )
    return jax.shard_map(
        per_device,
        mesh=mesh,
        in_specs=placed,
        out_specs=(P("dp", "region", None), P()),
        check_vma=False,
    )
```

```python
import functools
import math

import jax
import jax.numpy as jnp
from jax import lax
from jax.sharding import PartitionSpec as P

from jax.experimental import pallas as pl
from jax.experimental.pallas import tpu as pltpu

MESH_IDS = pl.DeviceIdType.MESH
COLOR_ORDERS = (("z", "y", "x"), ("y", "x", "z"), ("x", "z", "y"))
CHUNK_ROWS = 24
COLOR_ROWS = 128 * CHUNK_ROWS
PAD_OFFSETS = 36


def coords_here():
    r = lax.axis_index("region")
    return {"x": lax.axis_index("dp"), "y": r // 8, "z": (r // 2) % 4, "core": r % 2}


def peer_of(at, dim, shift):
    x, y, z, c = at["x"], at["y"], at["z"], at["core"]
    if dim == "x":
        x = (x + shift) % 4
    elif dim == "y":
        y = (y + shift) % 4
    elif dim == "z":
        z = (z + shift) % 4
    else:
        c = 1 - c
    return (x, (y * 4 + z) * 2 + c)


def peer_multi(at, shifts):
    x, y, z, c = at["x"], at["y"], at["z"], at["core"]
    x = (x + shifts.get("x", 0)) % 4
    y = (y + shifts.get("y", 0)) % 4
    z = (z + shifts.get("z", 0)) % 4
    return (x, (y * 4 + z) * 2 + c)


PLANE_SHIFTS = [(sb, se) for sb in range(4) for se in range(4) if (sb, se) != (0, 0)]


def add_rows(dst, first, others, rows, slab):
    def body(i, carry):
        at = pl.ds(pl.multiple_of(i * slab, slab), slab)
        total = first(at)
        for other in others:
            total = total + other(at)
        dst(at, total)
        return carry

    lax.fori_loop(0, rows // slab, body, 0)


def allreduce_kernel(scale, x_ref, out_ref, rcore, part, r1, p1, r2, p2, r3, red, r23,
                     core_send, core_recv, rs_send, rs_recv, ag_send, ag_recv, agc_send, agc_recv, out_sem,
                     pl_send, pl_recv, pg_send, pg_recv):
    at = coords_here()
    half = COLOR_ROWS // 2
    barrier = pltpu.get_barrier_semaphore()
    shift_sets = {(("x", 0), ("y", 0), ("z", 0))}
    for order in COLOR_ORDERS:
        for s in (1, 2, 3):
            shift_sets.add(tuple(sorted({"x": 0, "y": 0, "z": 0, order[0]: s}.items())))
        for sb, se in PLANE_SHIFTS:
            shift_sets.add(tuple(sorted({"x": 0, "y": 0, "z": 0, order[1]: sb, order[2]: se}.items())))
    shift_sets.discard((("x", 0), ("y", 0), ("z", 0)))
    peers = [peer_of(at, "core", 1)] + [peer_multi(at, dict(s)) for s in sorted(shift_sets)]
    for p in peers:
        pl.semaphore_signal(barrier, inc=1, device_id=p, device_id_type=MESH_IDS)
    pl.semaphore_wait(barrier, len(peers))

    c = at["core"]
    copies = []
    for k in range(3):
        cp = pltpu.make_async_remote_copy(
            src_ref=x_ref.at[pl.ds(pl.multiple_of(k * COLOR_ROWS + (1 - c) * half, 8), half)],
            dst_ref=rcore.at[k], send_sem=core_send.at[k], recv_sem=core_recv.at[k],
            device_id=peer_of(at, "core", 1), device_id_type=MESH_IDS)
        cp.start()
        copies.append(cp)
    sources = (part, p1, p2)
    recvs = (r1, r2, r3)
    blocks = (COLOR_ROWS // 8, COLOR_ROWS // 32, COLOR_ROWS // 128)
    ranks = [[at[d] for d in order] for order in COLOR_ORDERS]

    def scatter_sends(stage, k):
        blk, src, rbuf = blocks[stage], sources[stage], recvs[stage]
        dim, me = COLOR_ORDERS[k][stage], ranks[k][stage]
        row = []
        for s in (1, 2, 3):
            cp = pltpu.make_async_remote_copy(
                src_ref=src.at[k, pl.ds(pl.multiple_of(((me + s) % 4) * blk, 8), blk)],
                dst_ref=rbuf.at[k, s - 1], send_sem=rs_send.at[stage, k, s - 1],
                recv_sem=rs_recv.at[stage, k, s - 1],
                device_id=peer_of(at, dim, s), device_id_type=MESH_IDS)
            cp.start()
            row.append(cp)
        return row

    def gather_sends(step, k):
        stage = (2, 1, 0)[step]
        blk = (COLOR_ROWS // 128, COLOR_ROWS // 32, COLOR_ROWS // 8)[step]
        dim = COLOR_ORDERS[k][stage]
        a, b, e = ranks[k]
        lead = (c * 64 + a * 16 + b * 4 + e, c * 64 + a * 16 + b * 4, c * 64 + a * 16)[step]
        pos = pl.multiple_of(k * COLOR_ROWS + lead * CHUNK_ROWS, 8)
        row = []
        for s in (1, 2, 3):
            cp = pltpu.make_async_remote_copy(
                src_ref=out_ref.at[pl.ds(pos, blk)], dst_ref=out_ref.at[pl.ds(pos, blk)],
                send_sem=ag_send.at[stage, k, s - 1], recv_sem=ag_recv.at[stage, k, s - 1],
                device_id=peer_of(at, dim, s), device_id_type=MESH_IDS)
            cp.start()
            row.append(cp)
        return row

    def pair_send(k):
        pos = pl.multiple_of(k * COLOR_ROWS + c * half, 8)
        cp = pltpu.make_async_remote_copy(
            src_ref=out_ref.at[pl.ds(pos, half)], dst_ref=out_ref.at[pl.ds(pos, half)],
            send_sem=agc_send.at[k], recv_sem=agc_recv.at[k],
            device_id=peer_of(at, "core", 1), device_id_type=MESH_IDS)
        cp.start()
        return cp

    def plane_sends(k):
        a, b, e = ranks[k]
        order = COLOR_ORDERS[k]
        row = []
        for slot, (sb, se) in enumerate(PLANE_SHIFTS):
            chunk = ((b + sb) % 4) * 4 + (e + se) % 4
            cp = pltpu.make_async_remote_copy(
                src_ref=p1.at[k, pl.ds(pl.multiple_of(chunk * CHUNK_ROWS, 8), CHUNK_ROWS)],
                dst_ref=r23.at[k, slot], send_sem=pl_send.at[k, slot], recv_sem=pl_recv.at[k, slot],
                device_id=peer_multi(at, {order[1]: sb, order[2]: se}), device_id_type=MESH_IDS)
            cp.start()
            row.append(cp)
        return row

    def plane_gather(k):
        a, b, e = ranks[k]
        order = COLOR_ORDERS[k]
        pos = pl.multiple_of(k * COLOR_ROWS + (c * 64 + a * 16 + b * 4 + e) * CHUNK_ROWS, 8)
        row = []
        for slot, (sb, se) in enumerate(PLANE_SHIFTS):
            cp = pltpu.make_async_remote_copy(
                src_ref=out_ref.at[pl.ds(pos, CHUNK_ROWS)], dst_ref=out_ref.at[pl.ds(pos, CHUNK_ROWS)],
                send_sem=pg_send.at[k, slot], recv_sem=pg_recv.at[k, slot],
                device_id=peer_multi(at, {order[1]: sb, order[2]: se}), device_id_type=MESH_IDS)
            cp.start()
            row.append(cp)
        return row

    staged = [None] * 3
    for k in range(3):
        copies[k].wait()
        base = k * COLOR_ROWS + c * half
        add_rows(lambda a, v, k=k: part.__setitem__((k, a), v),
                 lambda a, base=base: x_ref[pl.ds(pl.multiple_of(base, 8) + a.start, a.size)],
                 [lambda a, k=k: rcore[k, a]], half, 128)
        staged[k] = scatter_sends(0, k)
    blk = blocks[0]
    for k in range(3):
        for cp in staged[k]:
            cp.wait()
        me = ranks[k][0]
        own = pl.multiple_of(me * blk, 8)
        others = [lambda a, k=k, j=j: r1[k, j, a] for j in range(3)]
        first = lambda a, k=k, own=own: part[k, pl.ds(own + a.start, a.size)]
        add_rows(lambda a, v, k=k: p1.__setitem__((k, a), v), first, others, blk, 128)
        staged[k] = plane_sends(k)
    for k in range(3):
        for cp in staged[k]:
            cp.wait()
        a, b, e = ranks[k]
        mine = pl.multiple_of((b * 4 + e) * CHUNK_ROWS, 8)
        total = p1[k, pl.ds(mine, CHUNK_ROWS)]
        for slot in range(len(PLANE_SHIFTS)):
            total = total + r23[k, slot]
        pos = pl.multiple_of(k * COLOR_ROWS + (c * 64 + a * 16 + b * 4 + e) * CHUNK_ROWS, 8)
        red[k] = total * scale
        put = pltpu.make_async_copy(red.at[k], out_ref.at[pl.ds(pos, CHUNK_ROWS)], out_sem.at[k])
        put.start()
        put.wait()
        staged[k] = plane_gather(k)
    for k in range(3):
        for cp in staged[k]:
            cp.wait()
        staged[k] = gather_sends(2, k)
    for k in range(3):
        for cp in staged[k]:
            cp.wait()
        staged[k] = [pair_send(k)]
    for k in range(3):
        for cp in staged[k]:
            cp.wait()

def summed_everywhere(stacked, scale):
    rows = PAD_OFFSETS * 256
    width = stacked.shape[2]
    data = jnp.concatenate(
        [stacked, jnp.zeros((PAD_OFFSETS - stacked.shape[0],) + stacked.shape[1:], stacked.dtype)], 0
    ).reshape(rows, width)
    f32 = jnp.float32
    blocks = (COLOR_ROWS // 8, COLOR_ROWS // 32, COLOR_ROWS // 128)
    total = pl.pallas_call(
        functools.partial(allreduce_kernel, scale),
        out_shape=jax.ShapeDtypeStruct((rows, width), f32),
        in_specs=[pl.BlockSpec(memory_space=pltpu.VMEM)],
        out_specs=pl.BlockSpec(memory_space=pl.ANY),
        scratch_shapes=[
            pltpu.VMEM((3, COLOR_ROWS // 2, width), f32),
            pltpu.VMEM((3, COLOR_ROWS // 2, width), f32),
            pltpu.VMEM((3, 3, blocks[0], width), f32),
            pltpu.VMEM((3, blocks[0], width), f32),
            pltpu.VMEM((3, 3, blocks[1], width), f32),
            pltpu.VMEM((3, blocks[1], width), f32),
            pltpu.VMEM((3, 3, blocks[2], width), f32),
            pltpu.VMEM((3, blocks[2], width), f32),
            pltpu.VMEM((3, 15, CHUNK_ROWS, width), f32),
            pltpu.SemaphoreType.DMA((3,)),
            pltpu.SemaphoreType.DMA((3,)),
            pltpu.SemaphoreType.DMA((3, 3, 3)),
            pltpu.SemaphoreType.DMA((3, 3, 3)),
            pltpu.SemaphoreType.DMA((3, 3, 3)),
            pltpu.SemaphoreType.DMA((3, 3, 3)),
            pltpu.SemaphoreType.DMA((3,)),
            pltpu.SemaphoreType.DMA((3,)),
            pltpu.SemaphoreType.DMA((3,)),
            pltpu.SemaphoreType.DMA((3, 15)),
            pltpu.SemaphoreType.DMA((3, 15)),
            pltpu.SemaphoreType.DMA((3, 15)),
            pltpu.SemaphoreType.DMA((3, 15)),
        ],
        compiler_params=pltpu.CompilerParams(
            collective_id=0, has_side_effects=True, vmem_limit_bytes=64 * 1024 * 1024
        ),
    )(data)
    return total[: stacked.shape[0] * stacked.shape[1]].reshape(stacked.shape)


def passed_along(array, axis, by):
    peers = lax.axis_size(axis)
    pairs = [(i, i + by) for i in range(peers) if 0 <= i + by < peers]
    return lax.ppermute(array, axis, pairs)


def contract_rows(left, right):
    return lax.dot_general(
        left, right, (((0,), (0,)), ((), ())), preferred_element_type=jnp.float32
    )


def through_kernel(grads, kernel):
    return lax.dot_general(
        grads, kernel, (((1,), (1,)), ((), ())), preferred_element_type=jnp.float32
    )


def one_hot_rows(lists, rows_here):
    numbers = lax.broadcasted_iota(jnp.int32, lists.shape + (rows_here,), lists.ndim)
    return (lists[..., None] == numbers).astype(jnp.bfloat16)


def pick_rows(table, source):
    return jnp.einsum("...v,vc->...c", table, source, preferred_element_type=jnp.float32).astype(
        jnp.bfloat16
    )


def place_rows(table, rows):
    return jnp.einsum("fbv,fbc->vc", table, rows, preferred_element_type=jnp.float32)


def face_products(features, grads, kernels):
    weight_grad = jnp.einsum("fbc,fbd->fcd", features, grads, preferred_element_type=jnp.float32)
    out_rows = jnp.einsum(
        "fbd,fcd->fbc", grads, kernels, preferred_element_type=jnp.float32
    ).astype(jnp.bfloat16)
    return (weight_grad, out_rows)


def per_device(feats, grad_out, weight, loc_in, loc_out, bnd_out, bnd_in):
    rows_here = feats.shape[1]
    pairs = loc_in.shape[3]
    own_feat = feats[0]
    own_grad = grad_out[0]
    center = contract_rows(own_feat, own_grad)
    accumulated = through_kernel(own_grad, weight[13])
    table_in = one_hot_rows(loc_in[0, 0], rows_here)
    table_out = one_hot_rows(loc_out[0, 0], rows_here)
    gathered_x = pick_rows(table_in, own_feat)
    gathered_g = pick_rows(table_out, own_grad)
    placed = jnp.einsum(
        "kpv,kpc->vkc", table_in, gathered_g, preferred_element_type=jnp.float32
    ).astype(jnp.bfloat16)
    side_kernels = jnp.concatenate([weight[0:13], weight[14:27]], 0)
    accumulated = accumulated + jnp.einsum(
        "vkd,kcd->vc", placed, side_kernels, preferred_element_type=jnp.float32
    )
    offset_grads = jnp.einsum(
        "kpc,kpd->kcd", gathered_x, gathered_g, preferred_element_type=jnp.float32
    )
    low_kernels = weight[0:9]
    high_kernels = weight[18:27]
    face_out_table = one_hot_rows(bnd_out[0, 0], rows_here)
    face_in_table = one_hot_rows(bnd_in[0, 0], rows_here)
    own_grads = pick_rows(face_out_table, own_grad)
    asked = pick_rows(face_in_table, own_feat)
    from_below = passed_along(own_grads[1], "region", 1)
    from_above = passed_along(own_grads[0], "region", -1)
    high_grad, below_rows = face_products(asked[0], from_below, high_kernels)
    low_grad, above_rows = face_products(asked[1], from_above, low_kernels)
    accumulated = accumulated + place_rows(face_in_table[0], below_rows)
    accumulated = accumulated + place_rows(face_in_table[1], above_rows)
    stacked = jnp.concatenate(
        [
            offset_grads[0:9] + low_grad,
            offset_grads[9:13],
            center[None],
            offset_grads[13:17],
            offset_grads[17:26] + high_grad,
        ],
        0,
    )
    loss_scale = 1.0 / math.sqrt(pairs * lax.axis_size("dp") * lax.axis_size("region"))
    grad_weight = summed_everywhere(stacked, loss_scale)
    grad_input = accumulated.astype(jnp.bfloat16)[None]
    return (grad_input, grad_weight)


def solution(mesh):
    placed = (
        P("dp", "region", None),
        P("dp", "region", None),
        P(),
        P("dp", "region", None, None),
        P("dp", "region", None, None),
        P("dp", "region", None, None, None),
        P("dp", "region", None, None, None),
    )
    return jax.shard_map(
        per_device,
        mesh=mesh,
        in_specs=placed,
        out_specs=(P("dp", "region", None), P()),
        check_vma=False,
    )
```

```python
import functools
import math

import jax
import jax.numpy as jnp
from jax import lax
from jax.sharding import PartitionSpec as P

from jax.experimental import pallas as pl
from jax.experimental.pallas import tpu as pltpu

MESH_IDS = pl.DeviceIdType.MESH
COLOR_ORDERS = (("z", "y", "x"), ("y", "x", "z"), ("x", "z", "y"))
CHUNK_ROWS = 24
COLOR_ROWS = 128 * CHUNK_ROWS
PAD_OFFSETS = 36


def coords_here():
    r = lax.axis_index("region")
    return {"x": lax.axis_index("dp"), "y": r // 8, "z": (r // 2) % 4, "core": r % 2}


def peer_of(at, dim, shift):
    x, y, z, c = at["x"], at["y"], at["z"], at["core"]
    if dim == "x":
        x = (x + shift) % 4
    elif dim == "y":
        y = (y + shift) % 4
    elif dim == "z":
        z = (z + shift) % 4
    else:
        c = 1 - c
    return (x, (y * 4 + z) * 2 + c)


def add_rows(dst, first, others, rows, slab):
    def body(i, carry):
        at = pl.ds(pl.multiple_of(i * slab, slab), slab)
        total = first(at)
        for other in others:
            total = total + other(at)
        dst(at, total)
        return carry

    lax.fori_loop(0, rows // slab, body, 0)


def allreduce_kernel(scale, x_ref, out_ref, rcore, part, r1, p1, r2, p2, r3, red,
                     core_send, core_recv, rs_send, rs_recv, ag_send, ag_recv, agc_send, agc_recv, out_sem):
    at = coords_here()
    half = COLOR_ROWS // 2
    barrier = pltpu.get_barrier_semaphore()
    peers = [peer_of(at, "core", 1)] + [peer_of(at, d, s) for d in ("z", "y", "x") for s in (1, 2, 3)]
    for p in peers:
        pl.semaphore_signal(barrier, inc=1, device_id=p, device_id_type=MESH_IDS)
    pl.semaphore_wait(barrier, len(peers))

    c = at["core"]
    copies = []
    for k in range(3):
        cp = pltpu.make_async_remote_copy(
            src_ref=x_ref.at[pl.ds(pl.multiple_of(k * COLOR_ROWS + (1 - c) * half, 8), half)],
            dst_ref=rcore.at[k], send_sem=core_send.at[k], recv_sem=core_recv.at[k],
            device_id=peer_of(at, "core", 1), device_id_type=MESH_IDS)
        cp.start()
        copies.append(cp)
    sources = (part, p1, p2)
    recvs = (r1, r2, r3)
    blocks = (COLOR_ROWS // 8, COLOR_ROWS // 32, COLOR_ROWS // 128)
    ranks = [[at[d] for d in order] for order in COLOR_ORDERS]

    def scatter_sends(stage, k):
        blk, src, rbuf = blocks[stage], sources[stage], recvs[stage]
        dim, me = COLOR_ORDERS[k][stage], ranks[k][stage]
        row = []
        for s in (1, 2, 3):
            cp = pltpu.make_async_remote_copy(
                src_ref=src.at[k, pl.ds(pl.multiple_of(((me + s) % 4) * blk, 8), blk)],
                dst_ref=rbuf.at[k, s - 1], send_sem=rs_send.at[stage, k, s - 1],
                recv_sem=rs_recv.at[stage, k, s - 1],
                device_id=peer_of(at, dim, s), device_id_type=MESH_IDS)
            cp.start()
            row.append(cp)
        return row

    def gather_sends(step, k):
        stage = (2, 1, 0)[step]
        blk = (COLOR_ROWS // 128, COLOR_ROWS // 32, COLOR_ROWS // 8)[step]
        dim = COLOR_ORDERS[k][stage]
        a, b, e = ranks[k]
        lead = (c * 64 + a * 16 + b * 4 + e, c * 64 + a * 16 + b * 4, c * 64 + a * 16)[step]
        pos = pl.multiple_of(k * COLOR_ROWS + lead * CHUNK_ROWS, 8)
        row = []
        for s in (1, 2, 3):
            cp = pltpu.make_async_remote_copy(
                src_ref=out_ref.at[pl.ds(pos, blk)], dst_ref=out_ref.at[pl.ds(pos, blk)],
                send_sem=ag_send.at[stage, k, s - 1], recv_sem=ag_recv.at[stage, k, s - 1],
                device_id=peer_of(at, dim, s), device_id_type=MESH_IDS)
            cp.start()
            row.append(cp)
        return row

    def pair_send(k):
        pos = pl.multiple_of(k * COLOR_ROWS + c * half, 8)
        cp = pltpu.make_async_remote_copy(
            src_ref=out_ref.at[pl.ds(pos, half)], dst_ref=out_ref.at[pl.ds(pos, half)],
            send_sem=agc_send.at[k], recv_sem=agc_recv.at[k],
            device_id=peer_of(at, "core", 1), device_id_type=MESH_IDS)
        cp.start()
        return cp

    staged = [None] * 3
    for k in range(3):
        copies[k].wait()
        base = k * COLOR_ROWS + c * half
        add_rows(lambda a, v, k=k: part.__setitem__((k, a), v),
                 lambda a, base=base: x_ref[pl.ds(pl.multiple_of(base, 8) + a.start, a.size)],
                 [lambda a, k=k: rcore[k, a]], half, 128)
        staged[k] = scatter_sends(0, k)
    for stage in range(3):
        blk, src, rbuf = blocks[stage], sources[stage], recvs[stage]
        for k in range(3):
            for cp in staged[k]:
                cp.wait()
            me = ranks[k][stage]
            own = pl.multiple_of(me * blk, 8)
            others = [lambda a, k=k, j=j, rbuf=rbuf: rbuf[k, j, a] for j in range(3)]
            first = lambda a, k=k, own=own, src=src: src[k, pl.ds(own + a.start, a.size)]
            if stage == 0:
                add_rows(lambda a, v, k=k: p1.__setitem__((k, a), v), first, others, blk, 128)
                staged[k] = scatter_sends(1, k)
            elif stage == 1:
                add_rows(lambda a, v, k=k: p2.__setitem__((k, a), v), first, others, blk, blk)
                staged[k] = scatter_sends(2, k)
            else:
                total = first(pl.ds(0, blk)) + others[0](pl.ds(0, blk)) + others[1](pl.ds(0, blk)) + others[2](pl.ds(0, blk))
                a, b, e = ranks[k]
                pos = pl.multiple_of(k * COLOR_ROWS + (c * 64 + a * 16 + b * 4 + e) * CHUNK_ROWS, 8)
                red[k] = total * scale
                put = pltpu.make_async_copy(red.at[k], out_ref.at[pl.ds(pos, blk)], out_sem.at[k])
                put.start()
                put.wait()
                staged[k] = gather_sends(0, k)
    for step in range(3):
        for k in range(3):
            for cp in staged[k]:
                cp.wait()
            staged[k] = gather_sends(step + 1, k) if step < 2 else [pair_send(k)]
    for k in range(3):
        for cp in staged[k]:
            cp.wait()

def summed_everywhere(stacked, scale):
    rows = PAD_OFFSETS * 256
    width = stacked.shape[2]
    data = jnp.concatenate(
        [stacked, jnp.zeros((PAD_OFFSETS - stacked.shape[0],) + stacked.shape[1:], stacked.dtype)], 0
    ).reshape(rows, width)
    f32 = jnp.float32
    blocks = (COLOR_ROWS // 8, COLOR_ROWS // 32, COLOR_ROWS // 128)
    total = pl.pallas_call(
        functools.partial(allreduce_kernel, scale),
        out_shape=jax.ShapeDtypeStruct((rows, width), f32),
        in_specs=[pl.BlockSpec(memory_space=pltpu.VMEM)],
        out_specs=pl.BlockSpec(memory_space=pl.ANY),
        scratch_shapes=[
            pltpu.VMEM((3, COLOR_ROWS // 2, width), f32),
            pltpu.VMEM((3, COLOR_ROWS // 2, width), f32),
            pltpu.VMEM((3, 3, blocks[0], width), f32),
            pltpu.VMEM((3, blocks[0], width), f32),
            pltpu.VMEM((3, 3, blocks[1], width), f32),
            pltpu.VMEM((3, blocks[1], width), f32),
            pltpu.VMEM((3, 3, blocks[2], width), f32),
            pltpu.VMEM((3, blocks[2], width), f32),
            pltpu.SemaphoreType.DMA((3,)),
            pltpu.SemaphoreType.DMA((3,)),
            pltpu.SemaphoreType.DMA((3, 3, 3)),
            pltpu.SemaphoreType.DMA((3, 3, 3)),
            pltpu.SemaphoreType.DMA((3, 3, 3)),
            pltpu.SemaphoreType.DMA((3, 3, 3)),
            pltpu.SemaphoreType.DMA((3,)),
            pltpu.SemaphoreType.DMA((3,)),
            pltpu.SemaphoreType.DMA((3,)),
        ],
        compiler_params=pltpu.CompilerParams(
            collective_id=0, has_side_effects=True, vmem_limit_bytes=64 * 1024 * 1024
        ),
    )(data)
    return total[: stacked.shape[0] * stacked.shape[1]].reshape(stacked.shape)


def face_kernel(up_ref, down_ref, below_ref, above_ref, got_below, got_above, sems):
    r = lax.axis_index("region")
    size = lax.axis_size("region")
    last = size - 1
    dp = lax.axis_index("dp")
    barrier = pltpu.get_barrier_semaphore()
    for near in (lax.rem(r + size - 1, size), lax.rem(r + 1, size)):
        pl.semaphore_signal(barrier, inc=1, device_id=(dp, near), device_id_type=MESH_IDS)
    pl.semaphore_wait(barrier, 2)

    upward = pltpu.make_async_remote_copy(
        src_ref=up_ref, dst_ref=got_below, send_sem=sems.at[0], recv_sem=sems.at[1],
        device_id=(dp, jnp.minimum(r + 1, last)), device_id_type=MESH_IDS)
    downward = pltpu.make_async_remote_copy(
        src_ref=down_ref, dst_ref=got_above, send_sem=sems.at[2], recv_sem=sems.at[3],
        device_id=(dp, jnp.maximum(r - 1, 0)), device_id_type=MESH_IDS)
    pl.when(r < last)(upward.start)
    pl.when(r > 0)(downward.start)
    pl.when(r < last)(upward.wait_send)
    pl.when(r > 0)(downward.wait_send)

    @pl.when(r > 0)
    def _():
        upward.wait_recv()
        below_ref[...] = got_below[...]

    @pl.when(r == 0)
    def _():
        below_ref[...] = jnp.zeros_like(below_ref)

    @pl.when(r < last)
    def _():
        downward.wait_recv()
        above_ref[...] = got_above[...]

    @pl.when(r == last)
    def _():
        above_ref[...] = jnp.zeros_like(above_ref)


def faces_exchanged(up, down):
    shape = jax.ShapeDtypeStruct(up.shape, up.dtype)
    return pl.pallas_call(
        face_kernel,
        out_shape=(shape, shape),
        in_specs=[pl.BlockSpec(memory_space=pltpu.VMEM)] * 2,
        out_specs=(pl.BlockSpec(memory_space=pltpu.VMEM),) * 2,
        scratch_shapes=[pltpu.VMEM(up.shape, up.dtype), pltpu.VMEM(up.shape, up.dtype),
                        pltpu.SemaphoreType.DMA((4,))],
        compiler_params=pltpu.CompilerParams(collective_id=1, has_side_effects=True),
    )(up, down)


def passed_along(array, axis, by):
    peers = lax.axis_size(axis)
    pairs = [(i, i + by) for i in range(peers) if 0 <= i + by < peers]
    return lax.ppermute(array, axis, pairs)


def contract_rows(left, right):
    return lax.dot_general(
        left, right, (((0,), (0,)), ((), ())), preferred_element_type=jnp.float32
    )


def through_kernel(grads, kernel):
    return lax.dot_general(
        grads, kernel, (((1,), (1,)), ((), ())), preferred_element_type=jnp.float32
    )


def one_hot_rows(lists, rows_here):
    numbers = lax.broadcasted_iota(jnp.int32, lists.shape + (rows_here,), lists.ndim)
    return (lists[..., None] == numbers).astype(jnp.bfloat16)


def pick_rows(table, source):
    return jnp.einsum("...v,vc->...c", table, source, preferred_element_type=jnp.float32).astype(
        jnp.bfloat16
    )


def place_rows(table, rows):
    return jnp.einsum("fbv,fbc->vc", table, rows, preferred_element_type=jnp.float32)


def face_products(features, grads, kernels):
    weight_grad = jnp.einsum("fbc,fbd->fcd", features, grads, preferred_element_type=jnp.float32)
    out_rows = jnp.einsum(
        "fbd,fcd->fbc", grads, kernels, preferred_element_type=jnp.float32
    ).astype(jnp.bfloat16)
    return (weight_grad, out_rows)


def per_device(feats, grad_out, weight, loc_in, loc_out, bnd_out, bnd_in):
    rows_here = feats.shape[1]
    pairs = loc_in.shape[3]
    own_feat = feats[0]
    own_grad = grad_out[0]
    center = contract_rows(own_feat, own_grad)
    accumulated = through_kernel(own_grad, weight[13])
    table_in = one_hot_rows(loc_in[0, 0], rows_here)
    table_out = one_hot_rows(loc_out[0, 0], rows_here)
    gathered_x = pick_rows(table_in, own_feat)
    gathered_g = pick_rows(table_out, own_grad)
    placed = jnp.einsum(
        "kpv,kpc->vkc", table_in, gathered_g, preferred_element_type=jnp.float32
    ).astype(jnp.bfloat16)
    side_kernels = jnp.concatenate([weight[0:13], weight[14:27]], 0)
    accumulated = accumulated + jnp.einsum(
        "vkd,kcd->vc", placed, side_kernels, preferred_element_type=jnp.float32
    )
    offset_grads = jnp.einsum(
        "kpc,kpd->kcd", gathered_x, gathered_g, preferred_element_type=jnp.float32
    )
    low_kernels = weight[0:9]
    high_kernels = weight[18:27]
    face_out_table = one_hot_rows(bnd_out[0, 0], rows_here)
    face_in_table = one_hot_rows(bnd_in[0, 0], rows_here)
    own_grads = pick_rows(face_out_table, own_grad)
    asked = pick_rows(face_in_table, own_feat)
    from_below, from_above = faces_exchanged(own_grads[1], own_grads[0])
    high_grad, below_rows = face_products(asked[0], from_below, high_kernels)
    low_grad, above_rows = face_products(asked[1], from_above, low_kernels)
    accumulated = accumulated + place_rows(face_in_table[0], below_rows)
    accumulated = accumulated + place_rows(face_in_table[1], above_rows)
    stacked = jnp.concatenate(
        [
            offset_grads[0:9] + low_grad,
            offset_grads[9:13],
            center[None],
            offset_grads[13:17],
            offset_grads[17:26] + high_grad,
        ],
        0,
    )
    loss_scale = 1.0 / math.sqrt(pairs * lax.axis_size("dp") * lax.axis_size("region"))
    grad_weight = summed_everywhere(stacked, loss_scale)
    grad_input = accumulated.astype(jnp.bfloat16)[None]
    return (grad_input, grad_weight)


def solution(mesh):
    placed = (
        P("dp", "region", None),
        P("dp", "region", None),
        P(),
        P("dp", "region", None, None),
        P("dp", "region", None, None),
        P("dp", "region", None, None, None),
        P("dp", "region", None, None, None),
    )
    return jax.shard_map(
        per_device,
        mesh=mesh,
        in_specs=placed,
        out_specs=(P("dp", "region", None), P()),
        check_vma=False,
    )
```

```python
import functools
import math

import jax
import jax.numpy as jnp
from jax import lax
from jax.sharding import PartitionSpec as P

from jax.experimental import pallas as pl
from jax.experimental.pallas import tpu as pltpu

MESH_IDS = pl.DeviceIdType.MESH
COLOR_ORDERS = (("z", "y", "x"), ("y", "x", "z"), ("x", "z", "y"))
CHUNK_ROWS = 24
COLOR_ROWS = 128 * CHUNK_ROWS
PAD_OFFSETS = 36


def coords_here():
    r = lax.axis_index("region")
    return {"x": lax.axis_index("dp"), "y": r // 8, "z": (r // 2) % 4, "core": r % 2}


def peer_of(at, dim, shift):
    x, y, z, c = at["x"], at["y"], at["z"], at["core"]
    if dim == "x":
        x = (x + shift) % 4
    elif dim == "y":
        y = (y + shift) % 4
    elif dim == "z":
        z = (z + shift) % 4
    else:
        c = 1 - c
    return (x, (y * 4 + z) * 2 + c)


def add_rows(dst, first, others, rows, slab):
    def body(i, carry):
        at = pl.ds(pl.multiple_of(i * slab, slab), slab)
        total = first(at)
        for other in others:
            total = total + other(at)
        dst(at, total)
        return carry

    lax.fori_loop(0, rows // slab, body, 0)


def allreduce_kernel(scale, x_ref, out_ref, rcore, part, r1, p1, r2, p2, r3, red,
                     core_send, core_recv, rs_send, rs_recv, ag_send, ag_recv, agc_send, agc_recv, out_sem):
    at = coords_here()
    half = COLOR_ROWS // 2
    barrier = pltpu.get_barrier_semaphore()
    peers = [peer_of(at, "core", 1)] + [peer_of(at, d, s) for d in ("z", "y", "x") for s in (1, 2, 3)]
    for p in peers:
        pl.semaphore_signal(barrier, inc=1, device_id=p, device_id_type=MESH_IDS)
    pl.semaphore_wait(barrier, len(peers))

    c = at["core"]
    copies = []
    for k in range(3):
        cp = pltpu.make_async_remote_copy(
            src_ref=x_ref.at[pl.ds(pl.multiple_of(k * COLOR_ROWS + (1 - c) * half, 8), half)],
            dst_ref=rcore.at[k], send_sem=core_send.at[k], recv_sem=core_recv.at[k],
            device_id=peer_of(at, "core", 1), device_id_type=MESH_IDS)
        cp.start()
        copies.append(cp)
    sources = (part, p1, p2)
    recvs = (r1, r2, r3)
    blocks = (COLOR_ROWS // 8, COLOR_ROWS // 32, COLOR_ROWS // 128)
    ranks = [[at[d] for d in order] for order in COLOR_ORDERS]

    def scatter_sends(stage, k):
        blk, src, rbuf = blocks[stage], sources[stage], recvs[stage]
        dim, me = COLOR_ORDERS[k][stage], ranks[k][stage]
        row = []
        for s in (1, 2, 3):
            cp = pltpu.make_async_remote_copy(
                src_ref=src.at[k, pl.ds(pl.multiple_of(((me + s) % 4) * blk, 8), blk)],
                dst_ref=rbuf.at[k, s - 1], send_sem=rs_send.at[stage, k, s - 1],
                recv_sem=rs_recv.at[stage, k, s - 1],
                device_id=peer_of(at, dim, s), device_id_type=MESH_IDS)
            cp.start()
            row.append(cp)
        return row

    def gather_sends(step, k):
        stage = (2, 1, 0)[step]
        blk = (COLOR_ROWS // 128, COLOR_ROWS // 32, COLOR_ROWS // 8)[step]
        dim = COLOR_ORDERS[k][stage]
        a, b, e = ranks[k]
        lead = (c * 64 + a * 16 + b * 4 + e, c * 64 + a * 16 + b * 4, c * 64 + a * 16)[step]
        pos = pl.multiple_of(k * COLOR_ROWS + lead * CHUNK_ROWS, 8)
        row = []
        for s in (1, 2, 3):
            cp = pltpu.make_async_remote_copy(
                src_ref=out_ref.at[pl.ds(pos, blk)], dst_ref=out_ref.at[pl.ds(pos, blk)],
                send_sem=ag_send.at[stage, k, s - 1], recv_sem=ag_recv.at[stage, k, s - 1],
                device_id=peer_of(at, dim, s), device_id_type=MESH_IDS)
            cp.start()
            row.append(cp)
        return row

    def pair_send(k):
        pos = pl.multiple_of(k * COLOR_ROWS + c * half, 8)
        cp = pltpu.make_async_remote_copy(
            src_ref=out_ref.at[pl.ds(pos, half)], dst_ref=out_ref.at[pl.ds(pos, half)],
            send_sem=agc_send.at[k], recv_sem=agc_recv.at[k],
            device_id=peer_of(at, "core", 1), device_id_type=MESH_IDS)
        cp.start()
        return cp

    staged = [None] * 3
    for k in range(3):
        copies[k].wait()
        base = k * COLOR_ROWS + c * half
        add_rows(lambda a, v, k=k: part.__setitem__((k, a), v),
                 lambda a, base=base: x_ref[pl.ds(pl.multiple_of(base, 8) + a.start, a.size)],
                 [lambda a, k=k: rcore[k, a]], half, 256)
        staged[k] = scatter_sends(0, k)
    for stage in range(3):
        blk, src, rbuf = blocks[stage], sources[stage], recvs[stage]
        for k in range(3):
            for cp in staged[k]:
                cp.wait()
            me = ranks[k][stage]
            own = pl.multiple_of(me * blk, 8)
            others = [lambda a, k=k, j=j, rbuf=rbuf: rbuf[k, j, a] for j in range(3)]
            first = lambda a, k=k, own=own, src=src: src[k, pl.ds(own + a.start, a.size)]
            if stage == 0:
                add_rows(lambda a, v, k=k: p1.__setitem__((k, a), v), first, others, blk, 192)
                staged[k] = scatter_sends(1, k)
            elif stage == 1:
                add_rows(lambda a, v, k=k: p2.__setitem__((k, a), v), first, others, blk, blk)
                staged[k] = scatter_sends(2, k)
            else:
                total = first(pl.ds(0, blk)) + others[0](pl.ds(0, blk)) + others[1](pl.ds(0, blk)) + others[2](pl.ds(0, blk))
                a, b, e = ranks[k]
                pos = pl.multiple_of(k * COLOR_ROWS + (c * 64 + a * 16 + b * 4 + e) * CHUNK_ROWS, 8)
                red[k] = total * scale
                put = pltpu.make_async_copy(red.at[k], out_ref.at[pl.ds(pos, blk)], out_sem.at[k])
                put.start()
                put.wait()
                staged[k] = gather_sends(0, k)
    for step in range(3):
        for k in range(3):
            for cp in staged[k]:
                cp.wait()
            staged[k] = gather_sends(step + 1, k) if step < 2 else [pair_send(k)]
    for k in range(3):
        for cp in staged[k]:
            cp.wait()

def summed_everywhere(stacked, scale):
    rows = PAD_OFFSETS * 256
    width = stacked.shape[2]
    data = jnp.concatenate(
        [stacked, jnp.zeros((PAD_OFFSETS - stacked.shape[0],) + stacked.shape[1:], stacked.dtype)], 0
    ).reshape(rows, width)
    f32 = jnp.float32
    blocks = (COLOR_ROWS // 8, COLOR_ROWS // 32, COLOR_ROWS // 128)
    total = pl.pallas_call(
        functools.partial(allreduce_kernel, scale),
        out_shape=jax.ShapeDtypeStruct((rows, width), f32),
        in_specs=[pl.BlockSpec(memory_space=pltpu.VMEM)],
        out_specs=pl.BlockSpec(memory_space=pl.ANY),
        scratch_shapes=[
            pltpu.VMEM((3, COLOR_ROWS // 2, width), f32),
            pltpu.VMEM((3, COLOR_ROWS // 2, width), f32),
            pltpu.VMEM((3, 3, blocks[0], width), f32),
            pltpu.VMEM((3, blocks[0], width), f32),
            pltpu.VMEM((3, 3, blocks[1], width), f32),
            pltpu.VMEM((3, blocks[1], width), f32),
            pltpu.VMEM((3, 3, blocks[2], width), f32),
            pltpu.VMEM((3, blocks[2], width), f32),
            pltpu.SemaphoreType.DMA((3,)),
            pltpu.SemaphoreType.DMA((3,)),
            pltpu.SemaphoreType.DMA((3, 3, 3)),
            pltpu.SemaphoreType.DMA((3, 3, 3)),
            pltpu.SemaphoreType.DMA((3, 3, 3)),
            pltpu.SemaphoreType.DMA((3, 3, 3)),
            pltpu.SemaphoreType.DMA((3,)),
            pltpu.SemaphoreType.DMA((3,)),
            pltpu.SemaphoreType.DMA((3,)),
        ],
        compiler_params=pltpu.CompilerParams(
            collective_id=0, has_side_effects=True, vmem_limit_bytes=64 * 1024 * 1024
        ),
    )(data)
    return total[: stacked.shape[0] * stacked.shape[1]].reshape(stacked.shape)


def passed_along(array, axis, by):
    peers = lax.axis_size(axis)
    pairs = [(i, i + by) for i in range(peers) if 0 <= i + by < peers]
    return lax.ppermute(array, axis, pairs)


def contract_rows(left, right):
    return lax.dot_general(
        left, right, (((0,), (0,)), ((), ())), preferred_element_type=jnp.float32
    )


def through_kernel(grads, kernel):
    return lax.dot_general(
        grads, kernel, (((1,), (1,)), ((), ())), preferred_element_type=jnp.float32
    )


def one_hot_rows(lists, rows_here):
    numbers = lax.broadcasted_iota(jnp.int32, lists.shape + (rows_here,), lists.ndim)
    return (lists[..., None] == numbers).astype(jnp.bfloat16)


def pick_rows(table, source):
    return jnp.einsum("...v,vc->...c", table, source, preferred_element_type=jnp.float32).astype(
        jnp.bfloat16
    )


def place_rows(table, rows):
    return jnp.einsum("fbv,fbc->vc", table, rows, preferred_element_type=jnp.float32)


def face_products(features, grads, kernels):
    weight_grad = jnp.einsum("fbc,fbd->fcd", features, grads, preferred_element_type=jnp.float32)
    out_rows = jnp.einsum(
        "fbd,fcd->fbc", grads, kernels, preferred_element_type=jnp.float32
    ).astype(jnp.bfloat16)
    return (weight_grad, out_rows)


def per_device(feats, grad_out, weight, loc_in, loc_out, bnd_out, bnd_in):
    rows_here = feats.shape[1]
    pairs = loc_in.shape[3]
    own_feat = feats[0]
    own_grad = grad_out[0]
    center = contract_rows(own_feat, own_grad)
    accumulated = through_kernel(own_grad, weight[13])
    table_in = one_hot_rows(loc_in[0, 0], rows_here)
    table_out = one_hot_rows(loc_out[0, 0], rows_here)
    gathered_x = pick_rows(table_in, own_feat)
    gathered_g = pick_rows(table_out, own_grad)
    placed = jnp.einsum(
        "kpv,kpc->vkc", table_in, gathered_g, preferred_element_type=jnp.float32
    ).astype(jnp.bfloat16)
    side_kernels = jnp.concatenate([weight[0:13], weight[14:27]], 0)
    accumulated = accumulated + jnp.einsum(
        "vkd,kcd->vc", placed, side_kernels, preferred_element_type=jnp.float32
    )
    offset_grads = jnp.einsum(
        "kpc,kpd->kcd", gathered_x, gathered_g, preferred_element_type=jnp.float32
    )
    low_kernels = weight[0:9]
    high_kernels = weight[18:27]
    face_out_table = one_hot_rows(bnd_out[0, 0], rows_here)
    face_in_table = one_hot_rows(bnd_in[0, 0], rows_here)
    own_grads = pick_rows(face_out_table, own_grad)
    asked = pick_rows(face_in_table, own_feat)
    from_below = passed_along(own_grads[1], "region", 1)
    from_above = passed_along(own_grads[0], "region", -1)
    high_grad, below_rows = face_products(asked[0], from_below, high_kernels)
    low_grad, above_rows = face_products(asked[1], from_above, low_kernels)
    accumulated = accumulated + place_rows(face_in_table[0], below_rows)
    accumulated = accumulated + place_rows(face_in_table[1], above_rows)
    stacked = jnp.concatenate(
        [
            offset_grads[0:9] + low_grad,
            offset_grads[9:13],
            center[None],
            offset_grads[13:17],
            offset_grads[17:26] + high_grad,
        ],
        0,
    )
    loss_scale = 1.0 / math.sqrt(pairs * lax.axis_size("dp") * lax.axis_size("region"))
    grad_weight = summed_everywhere(stacked, loss_scale)
    grad_input = accumulated.astype(jnp.bfloat16)[None]
    return (grad_input, grad_weight)


def solution(mesh):
    placed = (
        P("dp", "region", None),
        P("dp", "region", None),
        P(),
        P("dp", "region", None, None),
        P("dp", "region", None, None),
        P("dp", "region", None, None, None),
        P("dp", "region", None, None, None),
    )
    return jax.shard_map(
        per_device,
        mesh=mesh,
        in_specs=placed,
        out_specs=(P("dp", "region", None), P()),
        check_vma=False,
    )
```
